512 devices in a mesh: dp: 128 (over x_hi, y, z), fsdp: 4 (over x_lo, core).
Axes of the slice: x: 4 (x_hi: 2, x_lo: 2; x = x_hi * 2 + x_lo), y: 4, z: 16, core: 2. Of those that a mesh axis runs over, the one named last changes fastest.
Arguments:
- tokens: bfloat16 [65536, 1280], P(('dp', 'fsdp')), may hold values from -3 to 3
- qkv_weight: bfloat16 [3, 1280, 1280], P(None, 'dp', 'fsdp'), may hold values from -1 to 1
- out_weight: bfloat16 [1280, 1280], P('fsdp', 'dp'), may hold values from -0.15625 to 0.15625
- merge_weight: bfloat16 [5120, 1280], P(('dp', 'fsdp')), may hold values from -0.078125 to 0.078125
- ln_gains: float32 [2, 1280], replicated, may hold values from 0.25 to 1.75
- segments: int32 [128, 512], P('dp', 'fsdp'), may hold values from 0 to 2, never falling along the last dimension, each value on 1 to 256 neighbouring positions
- merge_rows: int32 [512, 128], P(('dp', 'fsdp')), may hold values from 0 to 127, each once within a row
- owners: int32 [16384, 1], P(('dp', 'fsdp')), may hold values from 0 to 127; in each aligned block of 32 rows (0 to 31, 32 to 63, ...) at most 2 rows name the same one
Outputs:
- owned: bfloat16 [131072, 1280], P(('dp', 'fsdp'))
The draws below stay inside these ranges and needn't reach their ends.
Inputs may be any that keep to these rules, and one draw needn't show every extreme that they name: `segments`: within each row segment numbers never fall, every number appears, each request has 1 to 256 tokens and one has exactly 256. `merge_rows`: each row is a permutation of the device's local rows. `owners`: among the 32 merged tokens of one device no owner appears more than 2 times, and in some devices one appears exactly 2 times.
All inputs are finite; a program needn't handle non-finite values.
Results may differ from the reference program's by a relative error of at most 0.02.
Values may be sent and summed in bfloat16 or wider, within the bound.
A program may use at most 64 MiB of HBM per device.

```python
import math
import jax
import jax.numpy as jnp
import numpy as np
from jax import lax

D = 1280
HD = 80
MD = 1280
TOK_DEV = 128
SEGS = 3
QW = 1280
TOKENS = 65536
GROUP = 512
MERGED = 16384
CAP = 2
N_DP = 128
N_FSDP = 4


def draw_qkv_weight(key, part):
    base = jnp.clip(jax.random.normal(key, (3, D, QW), jnp.float32), -6.0, 6.0)
    chosen = jax.random.randint(jax.random.fold_in(key, 77), (2,), 0, N_DP)
    row_block = jnp.arange(D) // (D // N_DP)
    heavy = (row_block == chosen[0]) | (row_block == chosen[1])
    base = base * jnp.where(heavy, 4.0, 1.0)[None, :, None]
    return jnp.clip(base / math.sqrt(D), -1.0, 1.0).astype(jnp.bfloat16)


def block_levels(key, shape, cuts, least, largest):
    def one(dim, shards_of):
        heights = jax.random.uniform(jax.random.fold_in(jax.random.fold_in(key, 6), dim), (shards_of,), jnp.float32, least / len(cuts), largest / len(cuts))
        return jnp.repeat(jnp.exp(heights), shape[dim] // shards_of).reshape((-1,) + (1,) * (len(shape) - dim - 1))

    gain = one(*cuts[0])
    for cut in cuts[1:]:
        gain = gain * one(*cut)
    return gain


def profile(count, total, reach, skew):
    loads = [(1 << 20) // math.isqrt(rank ** skew) + 1 for rank in range(2, count + 1)]
    rest, given = total - reach - (count - 1), [1] * (count - 1)
    while rest > 0:
        free = [i for i in range(count - 1) if given[i] < reach]
        whole, left = sum([loads[i] for i in free]), rest
        for i in free:
            addition = min(reach - given[i], max(1, left * loads[i] // whole), rest)
            given[i] = given[i] + addition
            rest = rest - addition
    return np.array([reach] + given)


def uneven_parts(stream_key, amount, total, limit, skew):
    if amount == 2:
        one = jax.random.randint(stream_key, (), max(1, total - limit), min(limit, total - 1) + 1)
        return jnp.stack([one, total - one])
    tallies = jnp.asarray(profile(amount, total, limit, skew), jnp.int32)
    twos = (amount - 1) // 2
    donor, sink = tallies[1:1 + 2 * twos:2], tallies[2:2 + 2 * twos:2]
    slack = jnp.minimum(donor - 1, limit - sink)
    shifted = jax.random.randint(jax.random.fold_in(stream_key, 1), (twos,), 0, 1 << 20) % (slack + 1)
    tallies = tallies.at[1:1 + 2 * twos:2].set(donor - shifted).at[2:2 + 2 * twos:2].set(sink + shifted)
    return tallies[jax.random.permutation(jax.random.fold_in(stream_key, 2), amount)]


def routed_block(stream_key, own, number, rows, amount, top, most, skew):
    ranking = jax.random.permutation(stream_key, amount)
    crowded, common = portions_of(amount, rows * top, most, skew, True), portions_of(amount, rows * top, most, skew, False)
    places = jnp.arange(amount)

    def named(sizes, turn):
        used = int((sizes > 0).sum())
        fixed = max(1, used // 4)
        moved = fixed + (places - fixed + turn * (used - fixed)) % max(1, amount - fixed)
        return jnp.zeros((amount,), jnp.int32).at[ranking[jnp.where(places < fixed, places, moved)]].set(jnp.asarray(sizes, jnp.int32))

    sizes = jnp.where(number % 4 == 0, named(crowded, number // 4), named(common, number - number // 4 - 1))
    mixed = jax.random.permutation(jax.random.fold_in(own, 3), amount)
    giver, taker = mixed[0:amount // 2 * 2:2], mixed[1:amount // 2 * 2:2]
    room = jnp.minimum(sizes[giver] - 1, most - sizes[taker]) // 2
    room = jnp.where((giver == ranking[0]) | (taker == ranking[0]) | (sizes[taker] == 0), 0, jnp.maximum(room, 0))
    moved = jax.random.randint(jax.random.fold_in(own, 4), (amount // 2,), 0, 1 << 20) % (room + 1)
    sizes = sizes.at[giver].add(-moved).at[taker].add(moved)
    items = jnp.searchsorted(jnp.cumsum(sizes), jnp.arange(rows * top), side="right").astype(jnp.int32)
    table = items.reshape(top, rows).T
    table = table[jax.random.permutation(jax.random.fold_in(own, 1), rows)]
    turn = jax.random.randint(jax.random.fold_in(own, 2), (rows, 1), 0, top)
    return jnp.take_along_axis(table, (jnp.arange(top)[None, :] + turn) % top, axis=1)


def portions_of(number_of, total, bound, skew, full):
    loads = [(1 << 20) // math.isqrt(grade ** skew) + 1 for grade in range(1, number_of + 1)]
    largest = bound if full else min(bound, max(-(-total // number_of), total * loads[0] // sum(loads)))
    least = 1 if total - largest >= number_of - 1 else 0
    counts, spare = [largest] + [least] * (number_of - 1), total - largest - least * (number_of - 1)
    while spare > 0:
        movable = [i for i in range(1, number_of) if counts[i] < largest] or [i for i in range(1, number_of) if counts[i] < bound]
        pool, left = sum([loads[i] for i in movable]), spare
        for i in movable:
            addition = min(bound - counts[i], max(1, left * loads[i] // pool), spare)
            counts[i] = counts[i] + addition
            spare = spare - addition
    return np.array(counts)


def noise(own_key, dims, scale, most, cuts=(), kind=jnp.bfloat16):
    values = scale * jax.random.normal(own_key, dims, jnp.float32)
    if cuts:
        values = values * block_levels(own_key, dims, cuts, -0.22, 0.18)
    return jnp.clip(values, -most, most).astype(kind)


def setup_inputs(seed: int = 0) -> dict:
    arg_keys = jax.random.split(jax.random.key(seed), 9)
    tokens = noise(arg_keys[0], (TOKENS, D), 0.5, 3.0, ((0, 512),))
    qkv_weight = draw_qkv_weight(jax.random.fold_in(arg_keys[8], 71), 0)
    out_weight = noise(arg_keys[2], (QW, D), QW ** -0.5, 0.15625, ((0, 4), (1, 128)))
    merge_weight = noise(arg_keys[3], (4 * D, MD), (4 * D) ** -0.5, 0.078125, ((0, 512),))
    ln_gains = jnp.clip(1.0 + 0.15 * jax.random.normal(arg_keys[4], (2, D), jnp.float32), 0.25, 1.75)
    segments = jax.vmap(lambda own: jnp.searchsorted(jnp.cumsum(uneven_parts(own, SEGS, GROUP, 2 * TOK_DEV, 1)), jnp.arange(GROUP), side="right"))(jax.random.split(arg_keys[5], N_DP)).reshape((N_DP, GROUP)).astype(jnp.int32)
    merge_rows = jax.vmap(lambda own: jax.random.permutation(own, TOK_DEV))(jax.random.split(arg_keys[6], (N_DP * N_FSDP))).reshape((N_DP * N_FSDP, TOK_DEV)).astype(jnp.int32)
    owners_keys = jax.random.split(jax.random.fold_in(arg_keys[7], 1), MERGED // (TOK_DEV // 4))
    owners_turns = jax.random.permutation(jax.random.fold_in(arg_keys[7], 3), MERGED // (TOK_DEV // 4))
    owners = jax.vmap(lambda own, number: routed_block(jax.random.fold_in(arg_keys[7], 2), own, number, TOK_DEV // 4, N_DP, 1, CAP, 2))(owners_keys, owners_turns).reshape((MERGED, 1))
    return {"tokens": tokens, "qkv_weight": qkv_weight, "out_weight": out_weight, "merge_weight": merge_weight, "ln_gains": ln_gains, "segments": segments, "merge_rows": merge_rows, "owners": owners}


epsilon = 1e-06

def normalize(values_in, gain_row):
    widened = values_in.astype(jnp.float32)
    centered = widened - lax.optimization_barrier(jnp.mean(widened, axis=1, keepdims=True))
    variance = lax.optimization_barrier(jnp.mean(centered * centered, axis=1, keepdims=True))
    return (centered / jnp.sqrt(variance + epsilon) * gain_row).astype(jnp.bfloat16)

def attend(queries, keys_all, values_all, seg_rows, seg_cols):
    factor = 1.0 / math.sqrt(HD)
    allowed = seg_rows[:, None] == seg_cols[None, :]
    pieces = []
    for head_index in range(queries.shape[1] // HD):
        first_col = head_index * HD
        last_col = first_col + HD
        scores = jnp.dot(queries[:, first_col:last_col], keys_all[:, first_col:last_col].T, preferred_element_type=jnp.float32) * factor
        masked = jnp.where(allowed, scores, -jnp.inf)
        highest = lax.optimization_barrier(jnp.max(masked, axis=1, keepdims=True))
        weights = jnp.exp(masked - highest)
        totals = lax.optimization_barrier(jnp.sum(weights, axis=1, keepdims=True))
        head_out = jnp.dot(weights.astype(jnp.bfloat16), values_all[:, first_col:last_col], preferred_element_type=jnp.float32)
        pieces.append(head_out / totals)
    return jnp.concatenate(pieces, axis=1).astype(jnp.bfloat16)

def pack_lists(rows_block, targets):
    onehot = (targets[:, None] == jnp.arange(N_DP, dtype=jnp.int32)[None, :]).astype(jnp.int32)
    earlier = (jnp.cumsum(onehot, axis=0) - onehot).astype(jnp.int32)
    position = lax.optimization_barrier(jnp.sum(earlier * onehot, axis=1)).astype(jnp.int32)
    slot_index = targets * CAP + position
    placing = (jnp.arange(N_DP * CAP, dtype=jnp.int32)[:, None] == slot_index[None, :]).astype(jnp.bfloat16)
    return jnp.dot(placing, rows_block, preferred_element_type=jnp.float32).astype(jnp.bfloat16)

def reference(tokens, qkv_weight, out_weight, merge_weight, ln_gains, segments, merge_rows, owners):

    def one_group(operands):
        group_tokens, group_segs = operands
        normed = normalize(group_tokens, ln_gains[0])
        queries = jnp.dot(normed, qkv_weight[0], preferred_element_type=jnp.float32).astype(jnp.bfloat16)
        keys_all = jnp.dot(normed, qkv_weight[1], preferred_element_type=jnp.float32).astype(jnp.bfloat16)
        values_all = jnp.dot(normed, qkv_weight[2], preferred_element_type=jnp.float32).astype(jnp.bfloat16)
        attended = attend(queries, keys_all, values_all, group_segs, group_segs)
        update = jnp.dot(attended, out_weight, preferred_element_type=jnp.float32)
        layer_out = (group_tokens.astype(jnp.float32) + update).astype(jnp.bfloat16)
        return normalize(layer_out, ln_gains[1])
    merge_in = lax.map(one_group, (tokens.reshape(N_DP, N_FSDP * TOK_DEV, D), segments))
    merge_in = merge_in.reshape(N_DP * N_FSDP, TOK_DEV, D)
    stacked = jax.vmap(lambda rows_block, row_order: jnp.take(rows_block, row_order, axis=0))(merge_in, merge_rows)
    stacked = stacked.reshape(MERGED, 4 * D)
    merged = jnp.dot(stacked, merge_weight, preferred_element_type=jnp.float32).astype(jnp.bfloat16)
    packed = jax.vmap(pack_lists)(merged.reshape(N_DP * N_FSDP, TOK_DEV // 4, MD), owners.reshape(N_DP * N_FSDP, TOK_DEV // 4))
    packed = packed.reshape(N_DP, N_FSDP, N_DP, CAP, MD).transpose(2, 1, 0, 3, 4)
    return packed.reshape(N_DP * N_FSDP * N_DP * CAP, MD)
```

```python
import functools
import math

import jax
import jax.numpy as jnp
from jax import lax
from jax.experimental import pallas as pl
from jax.experimental.pallas import tpu as pltpu
from jax.sharding import PartitionSpec as P

HD = 80
NZ = 16
NY = 4
CH = 5
CW = 256
MESH = pl.DeviceIdType.MESH


def coords():
    dp = lax.axis_index("dp")
    fs = lax.axis_index("fsdp")
    return dp // 64, (dp // 16) % 4, dp % 16, fs


def deliver_kernel(
    merged_ref, slots_ref, out_ref, rows, keys, picked, landed, zs_send, zs_recv, ks_send, ks_recv, p_send, p_recv
):
    xh, y, z, fs = coords()
    plane = xh * 64 + y * 16
    mine = xh * 4 + y
    up = plane + (z + 1) % NZ
    down = plane + (z + NZ - 1) % NZ

    barrier = pltpu.get_barrier_semaphore()
    for peer in (up, down):
        pl.semaphore_signal(barrier, inc=1, device_id=(peer, fs), device_id_type=MESH)
    for step in range(1, 8):
        other = (mine + step) % 8
        pl.semaphore_signal(barrier, inc=1, device_id=(other * 16 + z, fs), device_id_type=MESH)
    for c in range(CH):
        rows[c, pl.ds(pl.multiple_of(z * 32, 32), 32), :] = merged_ref[:, c * CW : (c + 1) * CW]
    keys[z] = slots_ref[...]
    pl.semaphore_wait(barrier, 9)

    def key_copy(way, step):
        src = (z + NZ - (step - 1)) % NZ if way == 0 else (z + step - 1) % NZ
        return pltpu.make_async_remote_copy(
            src_ref=keys.at[src],
            dst_ref=keys.at[src],
            send_sem=ks_send.at[way, step - 1],
            recv_sem=ks_recv.at[way, step - 1],
            device_id=(up if way == 0 else down, fs),
            device_id_type=MESH,
        )

    def row_copy(c, way, step):
        src = (z + NZ - (step - 1)) % NZ if way == 0 else (z + step - 1) % NZ
        piece = rows.at[c, pl.ds(pl.multiple_of(src * 32, 32), 32), :]
        return pltpu.make_async_remote_copy(
            src_ref=piece,
            dst_ref=piece,
            send_sem=zs_send.at[c, way, step - 1],
            recv_sem=zs_recv.at[c, way, step - 1],
            device_id=(up if way == 0 else down, fs),
            device_id_type=MESH,
        )

    def row_arrival(c, way, step):
        src = (z + NZ - step) % NZ if way == 0 else (z + step) % NZ
        piece = rows.at[c, pl.ds(pl.multiple_of(src * 32, 32), 32), :]
        return pltpu.make_async_remote_copy(
            src_ref=piece,
            dst_ref=piece,
            send_sem=zs_send.at[c, way, step - 1],
            recv_sem=zs_recv.at[c, way, step - 1],
            device_id=(up if way == 0 else down, fs),
            device_id_type=MESH,
        )

    def key_arrival(way, step):
        src = (z + NZ - step) % NZ if way == 0 else (z + step) % NZ
        return pltpu.make_async_remote_copy(
            src_ref=keys.at[src],
            dst_ref=keys.at[src],
            send_sem=ks_send.at[way, step - 1],
            recv_sem=ks_recv.at[way, step - 1],
            device_id=(up if way == 0 else down, fs),
            device_id_type=MESH,
        )

    def plane_copy(c, step):
        other = (mine + step) % 8
        return pltpu.make_async_remote_copy(
            src_ref=picked.at[c, pl.ds(pl.multiple_of(other * 32, 32), 32), :],
            dst_ref=landed.at[c, pl.ds(pl.multiple_of(mine * 32, 32), 32), :],
            send_sem=p_send.at[c, step - 1],
            recv_sem=p_recv.at[c, step - 1],
            device_id=(other * 16 + z, fs),
            device_id_type=MESH,
        )

    def plane_arrival(c, step):
        other = (mine + 8 - step) % 8
        return pltpu.make_async_remote_copy(
            src_ref=picked.at[c, pl.ds(pl.multiple_of(other * 32, 32), 32), :],
            dst_ref=landed.at[c, pl.ds(pl.multiple_of(other * 32, 32), 32), :],
            send_sem=p_send.at[c, step - 1],
            recv_sem=p_recv.at[c, step - 1],
            device_id=(other * 16 + z, fs),
            device_id_type=MESH,
        )

    last = (8, 7)
    key_copy(0, 1).start()
    key_copy(1, 1).start()
    for c in range(CH):
        for way in range(2):
            row_copy(c, way, 1).start()
    chosen = None
    for wave in range(1, 8 + CH):
        if wave <= 8:
            for way in range(2):
                if wave <= last[way]:
                    key_arrival(way, wave).wait_recv()
                    if wave < last[way]:
                        key_copy(way, wave + 1).start()
        for c in range(CH):
            step = wave - c
            for way in range(2):
                if 1 <= step <= last[way]:
                    row_arrival(c, way, step).wait_recv()
                    if step < last[way]:
                        row_copy(c, way, step + 1).start()
        c = wave - 8
        if c >= 0:
            if chosen is None:
                pieces = [
                    keys[4 * q, 0:1, :] + keys[4 * q + 1, 0:1, :] + keys[4 * q + 2, 0:1, :] + keys[4 * q + 3, 0:1, :]
                    for q in range(4)
                ]
                row_key = jnp.concatenate(pieces, axis=1)
                place = lax.broadcasted_iota(jnp.int32, (256, 512), 0)
                column = lax.broadcasted_iota(jnp.int32, (256, 512), 1)
                wanted = (place & 224) + 2 * z + (place & 1) + 1
                same = ((place >> 1) & 15) == (column >> 5)
                chosen = jnp.where(same & (row_key == wanted), 1.0, 0.0).astype(jnp.bfloat16)
            picked[c] = jnp.dot(chosen, rows[c], preferred_element_type=jnp.float32).astype(jnp.bfloat16)
            for step in range(1, 8):
                plane_copy(c, step).start()
    for c in range(CH):
        own = pl.ds(pl.multiple_of(mine * 32, 32), 32)
        landed[c, own, :] = picked[c, own, :]
        for step in range(1, 8):
            plane_arrival(c, step).wait_recv()
        out_ref[:, c * CW : (c + 1) * CW] = landed[c]
    for way in range(2):
        for step in range(1, last[way] + 1):
            key_copy(way, step).wait_send()
            for c in range(CH):
                row_copy(c, way, step).wait_send()
    for c in range(CH):
        for step in range(1, 8):
            plane_copy(c, step).wait_send()


def deliver(merged, slots):
    width = merged.shape[1]
    return pl.pallas_call(
        deliver_kernel,
        out_shape=jax.ShapeDtypeStruct((256, width), jnp.bfloat16),
        in_specs=[pl.BlockSpec(memory_space=pltpu.VMEM)] * 2,
        out_specs=pl.BlockSpec(memory_space=pltpu.VMEM),
        scratch_shapes=[
            pltpu.VMEM((CH, 512, CW), jnp.bfloat16),
            pltpu.VMEM((NZ, 8, 128), jnp.int32),
            pltpu.VMEM((CH, 256, CW), jnp.bfloat16),
            pltpu.VMEM((CH, 256, CW), jnp.bfloat16),
            pltpu.SemaphoreType.DMA((CH, 2, 8)),
            pltpu.SemaphoreType.DMA((CH, 2, 8)),
            pltpu.SemaphoreType.DMA((2, 8)),
            pltpu.SemaphoreType.DMA((2, 8)),
            pltpu.SemaphoreType.DMA((CH, 7)),
            pltpu.SemaphoreType.DMA((CH, 7)),
        ],
        compiler_params=pltpu.CompilerParams(collective_id=0, has_side_effects=True),
    )(merged, slots)


epsilon = 1e-06


def normalize(values_in, gain_row):
    widened = values_in.astype(jnp.float32)
    centered = widened - jnp.mean(widened, axis=1, keepdims=True)
    variance = jnp.mean(centered * centered, axis=1, keepdims=True)
    return (centered * lax.rsqrt(variance + epsilon) * gain_row).astype(jnp.bfloat16)


def attend(queries, keys_all, values_all, seg_rows, seg_cols):
    factor = 1.0 / math.sqrt(HD)
    allowed = seg_rows[:, None] == seg_cols[None, :]
    pieces = []
    for head_index in range(queries.shape[1] // HD):
        first_col = head_index * HD
        last_col = first_col + HD
        scores = (
            lax.dot_general(
                queries[:, first_col:last_col],
                keys_all[:, first_col:last_col],
                (((1,), (1,)), ((), ())),
                preferred_element_type=jnp.float32,
            )
            * factor
        )
        masked = jnp.where(allowed, scores, -jnp.inf)
        highest = jnp.max(masked, axis=1, keepdims=True)
        weights = jnp.exp(masked - highest)
        totals = jnp.sum(weights, axis=1, keepdims=True)
        head_out = jnp.dot(
            weights.astype(jnp.bfloat16),
            values_all[:, first_col:last_col],
            preferred_element_type=jnp.float32,
        )
        pieces.append(head_out / totals)
    return jnp.concatenate(pieces, axis=1).astype(jnp.bfloat16)


def per_device(
    tokens, qkv_weight, out_weight, merge_weight, ln_gains, segments, merge_rows, owners
):
    n_dp = lax.axis_size("dp")
    n_fsdp = lax.axis_size("fsdp")
    qkv_mine = lax.all_gather(qkv_weight, "dp", axis=1, tiled=True)
    out_mine = lax.all_gather(out_weight, "dp", axis=1, tiled=True)
    normed = normalize(tokens, ln_gains[0])
    group_normed, group_segs = (
        lax.all_gather(normed, "fsdp", axis=0, tiled=True),
        lax.all_gather(segments, "fsdp", axis=1, tiled=True),
    )
    queries = jnp.dot(group_normed, qkv_mine[0], preferred_element_type=jnp.float32).astype(
        jnp.bfloat16
    )
    keys_all = jnp.dot(group_normed, qkv_mine[1], preferred_element_type=jnp.float32).astype(
        jnp.bfloat16
    )
    values_all = jnp.dot(group_normed, qkv_mine[2], preferred_element_type=jnp.float32).astype(
        jnp.bfloat16
    )
    attended_mine = attend(queries, keys_all, values_all, group_segs[0], group_segs[0])
    attended_local = lax.all_to_all(attended_mine, "fsdp", split_axis=0, concat_axis=1, tiled=True)
    out_full = lax.all_gather(out_mine, "fsdp", axis=0, tiled=True)
    update = jnp.dot(attended_local, out_full, preferred_element_type=jnp.float32)
    layer_out = (tokens.astype(jnp.float32) + update).astype(jnp.bfloat16)
    merge_in = normalize(layer_out, ln_gains[1])
    merge_count = tokens.shape[0] // 4
    stacked = jnp.take(merge_in, merge_rows[0], axis=0).reshape(merge_count, 4 * merge_in.shape[1])
    slice_rows = merge_weight.shape[0]
    part_rows = lax.all_gather(merge_weight, "dp", axis=0, tiled=True)
    blocks = stacked.reshape(merge_count, n_dp, n_fsdp * slice_rows)
    received = lax.all_to_all(blocks, "fsdp", split_axis=2, concat_axis=0, tiled=True)
    gathered_inputs = received.reshape(n_fsdp * merge_count, n_dp * slice_rows)
    merged = lax.psum_scatter(
        jnp.dot(gathered_inputs, part_rows, preferred_element_type=jnp.float32).astype(
            jnp.bfloat16
        ),
        "fsdp",
        scatter_dimension=0,
        tiled=True,
    )
    targets = owners[:, 0]
    onehot = (targets[:, None] == jnp.arange(n_dp, dtype=jnp.int32)[None, :]).astype(jnp.int32)
    earlier = jnp.cumsum(onehot, axis=0) - onehot
    position = jnp.sum(earlier * onehot, axis=1)
    slot_row = targets * 2 + position + 1
    quarter = lax.axis_index("dp") % 4
    spread = jnp.where(jnp.arange(4)[:, None] == quarter, slot_row[None, :], 0).reshape(1, 128)
    return deliver(merged, jnp.broadcast_to(spread, (8, 128)))


def solution(mesh):
    return jax.shard_map(
        per_device,
        mesh=mesh,
        in_specs=(
            P(("dp", "fsdp"), None),
            P(None, "dp", "fsdp"),
            P("fsdp", "dp"),
            P(("dp", "fsdp"), None),
            P(),
            P("dp", "fsdp"),
            P(("dp", "fsdp"), None),
            P(("dp", "fsdp"), None),
        ),
        out_specs=P(("dp", "fsdp"), None),
        check_vma=False,
    )
```

```python
import math

import jax
import jax.numpy as jnp
from jax import lax
from jax.experimental import pallas as pl
from jax.experimental.pallas import tpu as pltpu
from jax.sharding import Mesh
from jax.sharding import PartitionSpec as P

HD = 80
NZ = 16
NY = 4
MESH = pl.DeviceIdType.MESH
XG = ("xh", "fsdp")
epsilon = 1e-06


def coords():
    yz = lax.axis_index("yz")
    return lax.axis_index("xh"), yz // NZ, yz % NZ, lax.axis_index("fsdp")


def rows_of(place, n):
    return pl.ds(pl.multiple_of(place * n, n), n)


def gather_kernel(
    q_in, o_in, m_in, normed_in, seg_in, wq, wo, wm, normed_all, seg_all,
    q_box, o_box, m_box, q_send, q_recv, o_send, o_recv, m_send, m_recv, n_send, n_recv, g_send, g_recv,
    zq_send, zq_recv, zo_send, zo_recv, zm_send, zm_recv, s_send, s_recv,
):
    xh, y, z, fs = coords()
    core = fs % 2
    xlo = fs // 2
    mine = xh * 4 + y
    member = xh * 4 + fs
    up, down = (z + 1) % NZ, (z + NZ - 1) % NZ

    def dev(xh_, y_, z_, fs_):
        return (xh_, y_ * NZ + z_, fs_)

    barrier = pltpu.get_barrier_semaphore()
    for peer in (up, down):
        pl.semaphore_signal(barrier, inc=1, device_id=dev(xh, y, peer, fs), device_id_type=MESH)
    for dx in range(2):
        for dy in range(4):
            for df in range(4):
                if dx or dy or df:
                    there = dev((xh + dx) % 2, (y + dy) % 4, z, (fs + df) % 4)
                    pl.semaphore_signal(barrier, inc=1, device_id=there, device_id_type=MESH)
    pl.semaphore_wait(barrier, 33)

    def copy(src, dst, ssem, rsem, where):
        return pltpu.make_async_remote_copy(
            src_ref=src, dst_ref=dst, send_sem=ssem, recv_sem=rsem, device_id=where, device_id_type=MESH
        )

    def q_copy(step):
        dx, dy = step // 4, step % 4
        oxh, oy = (xh + dx) % 2, (y + dy) % 4
        return copy(q_in.at[oxh], q_box.at[mine], q_send.at[step], q_recv.at[step], dev(oxh, oy, z, fs))

    def q_arrival(step):
        dx, dy = step // 4, step % 4
        oxh, oy = (xh + dx) % 2, (y + 4 - dy) % 4
        return copy(q_in.at[xh], q_box.at[oxh * 4 + oy], q_send.at[step], q_recv.at[step], dev(oxh, oy, z, fs))

    for step in range(1, 8):
        q_copy(step).start()
    q_box[mine] = q_in[xh]

    o_steps = [(dx, dl, dy) for dx in range(2) for dl in range(2) for dy in range(4)]

    def o_slot(c, d):
        return o_box.at[c, d]

    def o_copy(k):
        dx, dl, dy = o_steps[k]
        oxh, olo, oy = (xh + dx) % 2, (xlo + dl) % 2, (y + dy) % 4
        return copy(o_in, o_slot(core, mine), o_send.at[k], o_recv.at[core, k], dev(oxh, oy, z, olo * 2 + xlo))

    def o_arrival(c, k):
        dx, dl, dy = o_steps[k]
        oxh, oy = (xh + dx) % 2, (y + 4 - dy) % 4
        return copy(o_in, o_slot(c, oxh * 4 + oy), o_send.at[k], o_recv.at[c, k], dev(oxh, oy, z, core * 2 + c))

    def o_remote(k):
        dx, dl, dy = o_steps[k]
        if dx or dy:
            return None
        return (xlo + dl) % 2 * 2 + xlo != fs

    for k in range(16):
        cond = o_remote(k)
        if cond is None:
            o_copy(k).start()
        else:
            @pl.when(cond)
            def _():
                o_copy(k).start()

    @pl.when(xlo == core)
    def _():
        o_box[core, mine] = o_in[...]

    def m_copy(dy):
        return copy(m_in, m_box.at[fs], m_send.at[dy], m_recv.at[fs], dev(xh, (y + dy) % 4, z, y))

    def m_arrival(j):
        return copy(m_in, m_box.at[j], m_send.at[0], m_recv.at[j], dev(xh, fs, z, j))

    for dy in range(1, 4):
        m_copy(dy).start()

    @pl.when(fs != y)
    def _():
        m_copy(0).start()

    @pl.when(fs == y)
    def _():
        m_box[fs] = m_in[...]

    def n_pair(step, to):
        dx, df = step // 4, step % 4
        oxh = (xh + dx) % 2
        ofs = (fs + df) % 4 if to else (fs + 4 - df) % 4
        slot = member if to else oxh * 4 + ofs
        there = dev(oxh, y, z, ofs)
        return (
            copy(normed_in, normed_all.at[slot], n_send.at[step], n_recv.at[step], there),
            copy(seg_in, seg_all.at[slot], g_send.at[step], g_recv.at[step], there),
        )

    for step in range(1, 8):
        for one in n_pair(step, True):
            one.start()
    normed_all[member] = normed_in[...]
    seg_all[member] = seg_in[...]

    def ten(count, depth):
        place = lax.broadcasted_iota(jnp.int32, (count, depth), 0)
        column = lax.broadcasted_iota(jnp.int32, (count, depth), 1)
        tens = (place * 52429) >> 19
        return jnp.where(column == tens * 16 + (place - tens * 10), 1.0, 0.0).astype(jnp.bfloat16)

    def settle(picker, block):
        return jnp.dot(picker, block, preferred_element_type=jnp.float32).astype(jnp.bfloat16)

    pick80 = ten(80, 128)
    for step in range(1, 8):
        q_arrival(step).wait_recv()
    wq[z] = settle(pick80, q_box[...].reshape(128, 512))

    def ring(buf, ssem, rsem, way, step, arriving):
        gone = step if arriving else step - 1
        src = (z + NZ - gone) % NZ if way == 0 else (z + gone) % NZ
        where = dev(xh, y, up if way == 0 else down, fs)
        return copy(buf.at[src], buf.at[src], ssem.at[way, step - 1], rsem.at[way, step - 1], where)

    wo_mine = wo.at[core]
    streams = ((wq, zq_send, zq_recv), (wo_mine, zo_send, zo_recv), (wm, zm_send, zm_recv))
    for way in range(2):
        ring(*streams[0], way, 1, False).start()

    for c in range(2):
        for k in range(16):
            dx, dl, dy = o_steps[k]
            here = (core + dl) % 2 == xlo
            if dx or dy:
                cond = here
            else:
                cond = here & (core * 2 + c != fs)

            @pl.when(cond)
            def _():
                o_arrival(c, k).wait_recv()
    left = o_box[0].reshape(128, 384)
    right = o_box[1].reshape(128, 384)
    wo[core, z, :, 0:256] = settle(pick80, left[:, 0:256])
    wo[core, z, :, 256:384] = settle(pick80, left[:, 256:384] + right[:, 0:128])
    wo[core, z, :, 384:640] = settle(pick80, right[:, 128:384])
    for way in range(2):
        ring(*streams[1], way, 1, False).start()

    for j in range(4):
        @pl.when((j != fs) | (y != fs))
        def _():
            m_arrival(j).wait_recv()
    wm[z] = settle(ten(40, 64), m_box[...].reshape(64, 1280))
    for way in range(2):
        ring(*streams[2], way, 1, False).start()

    def share(place, slot):
        return copy(
            wo.at[core, place], wo.at[core, place], s_send.at[slot], s_recv.at[slot], dev(xh, y, z, xlo * 2 + 1 - core)
        )

    def shared(place, slot):
        return copy(
            wo.at[1 - core, place], wo.at[1 - core, place], s_send.at[slot], s_recv.at[slot],
            dev(xh, y, z, xlo * 2 + 1 - core),
        )

    share(z, 0).start()
    last = (8, 7)
    for step in range(1, 9):
        for index, stream in enumerate(streams):
            for way in range(2):
                if step <= last[way]:
                    ring(*stream, way, step, True).wait_recv()
                    if step < last[way]:
                        ring(*stream, way, step + 1, False).start()
                    if index == 1:
                        place = (z + NZ - step) % NZ if way == 0 else (z + step) % NZ
                        share(place, step + 8 * way).start()
    for step in range(1, 8):
        for one in n_pair(step, False):
            one.wait_recv()
    shared(z, 0).wait_recv()
    for way in range(2):
        for step in range(1, last[way] + 1):
            place = (z + NZ - step) % NZ if way == 0 else (z + step) % NZ
            shared(place, step + 8 * way).wait_recv()

    for step in range(1, 8):
        q_copy(step).wait_send()
        for one in n_pair(step, True):
            one.wait_send()
    for k in range(16):
        cond = o_remote(k)
        if cond is None:
            o_copy(k).wait_send()
        else:
            @pl.when(cond)
            def _():
                o_copy(k).wait_send()
    for dy in range(1, 4):
        m_copy(dy).wait_send()

    @pl.when(fs != y)
    def _():
        m_copy(0).wait_send()

    share(z, 0).wait_send()
    for way in range(2):
        for step in range(1, last[way] + 1):
            for stream in streams:
                ring(*stream, way, step, False).wait_send()
            place = (z + NZ - step) % NZ if way == 0 else (z + step) % NZ
            share(place, step + 8 * way).wait_send()


def gather_all(q_in, o_in, m_in, normed, seg):
    bf = jnp.bfloat16
    dma = pltpu.SemaphoreType.DMA
    return pl.pallas_call(
        gather_kernel,
        out_shape=[
            jax.ShapeDtypeStruct((NZ, 80, 512), bf),
            jax.ShapeDtypeStruct((2, NZ, 80, 640), bf),
            jax.ShapeDtypeStruct((NZ, 40, 1280), bf),
            jax.ShapeDtypeStruct((8, 128, 1280), bf),
            jax.ShapeDtypeStruct((8, 8, 128), jnp.int32),
        ],
        in_specs=[pl.BlockSpec(memory_space=pltpu.VMEM)] * 5,
        out_specs=[pl.BlockSpec(memory_space=pltpu.VMEM)] * 5,
        scratch_shapes=[
            pltpu.VMEM((8, 16, 512), bf),
            pltpu.VMEM((2, 8, 16, 384), bf),
            pltpu.VMEM((4, 16, 1280), bf),
            dma((8,)), dma((8,)), dma((16,)), dma((2, 16)), dma((4,)), dma((4,)),
            dma((8,)), dma((8,)), dma((8,)), dma((8,)),
            dma((2, 8)), dma((2, 8)), dma((2, 8)), dma((2, 8)), dma((2, 8)), dma((2, 8)),
            dma((17,)), dma((17,)),
        ],
        compiler_params=pltpu.CompilerParams(collective_id=1, has_side_effects=True),
    )(q_in, o_in, m_in, normed, seg)


CH = 5
CW = 256


def deliver_kernel(
    merged_ref, slots_ref, out_ref, rows, keys, picked, landed, zs_send, zs_recv, ks_send, ks_recv, p_send, p_recv
):
    xh, y, z, fs = coords()
    mine = xh * 4 + y
    up = y * NZ + (z + 1) % NZ
    down = y * NZ + (z + NZ - 1) % NZ

    barrier = pltpu.get_barrier_semaphore()
    for peer in (up, down):
        pl.semaphore_signal(barrier, inc=1, device_id=(xh, peer, fs), device_id_type=MESH)
    for step in range(1, 8):
        other = (mine + step) % 8
        pl.semaphore_signal(barrier, inc=1, device_id=(other // 4, other % 4 * NZ + z, fs), device_id_type=MESH)
    for c in range(CH):
        rows[c, pl.ds(pl.multiple_of(z * 32, 32), 32), :] = merged_ref[:, c * CW : (c + 1) * CW]
    keys[z] = slots_ref[...]
    pl.semaphore_wait(barrier, 9)

    def key_copy(way, step):
        src = (z + NZ - (step - 1)) % NZ if way == 0 else (z + step - 1) % NZ
        return pltpu.make_async_remote_copy(
            src_ref=keys.at[src],
            dst_ref=keys.at[src],
            send_sem=ks_send.at[way, step - 1],
            recv_sem=ks_recv.at[way, step - 1],
            device_id=(xh, up if way == 0 else down, fs),
            device_id_type=MESH,
        )

    def row_copy(c, way, step):
        src = (z + NZ - (step - 1)) % NZ if way == 0 else (z + step - 1) % NZ
        piece = rows.at[c, pl.ds(pl.multiple_of(src * 32, 32), 32), :]
        return pltpu.make_async_remote_copy(
            src_ref=piece,
            dst_ref=piece,
            send_sem=zs_send.at[c, way, step - 1],
            recv_sem=zs_recv.at[c, way, step - 1],
            device_id=(xh, up if way == 0 else down, fs),
            device_id_type=MESH,
        )

    def row_arrival(c, way, step):
        src = (z + NZ - step) % NZ if way == 0 else (z + step) % NZ
        piece = rows.at[c, pl.ds(pl.multiple_of(src * 32, 32), 32), :]
        return pltpu.make_async_remote_copy(
            src_ref=piece,
            dst_ref=piece,
            send_sem=zs_send.at[c, way, step - 1],
            recv_sem=zs_recv.at[c, way, step - 1],
            device_id=(xh, up if way == 0 else down, fs),
            device_id_type=MESH,
        )

    def key_arrival(way, step):
        src = (z + NZ - step) % NZ if way == 0 else (z + step) % NZ
        return pltpu.make_async_remote_copy(
            src_ref=keys.at[src],
            dst_ref=keys.at[src],
            send_sem=ks_send.at[way, step - 1],
            recv_sem=ks_recv.at[way, step - 1],
            device_id=(xh, up if way == 0 else down, fs),
            device_id_type=MESH,
        )

    def plane_copy(c, step):
        other = (mine + step) % 8
        return pltpu.make_async_remote_copy(
            src_ref=picked.at[c, pl.ds(pl.multiple_of(other * 32, 32), 32), :],
            dst_ref=landed.at[c, pl.ds(pl.multiple_of(mine * 32, 32), 32), :],
            send_sem=p_send.at[c, step - 1],
            recv_sem=p_recv.at[c, step - 1],
            device_id=(other // 4, other % 4 * NZ + z, fs),
            device_id_type=MESH,
        )

    def plane_arrival(c, step):
        other = (mine + 8 - step) % 8
        return pltpu.make_async_remote_copy(
            src_ref=picked.at[c, pl.ds(pl.multiple_of(other * 32, 32), 32), :],
            dst_ref=landed.at[c, pl.ds(pl.multiple_of(other * 32, 32), 32), :],
            send_sem=p_send.at[c, step - 1],
            recv_sem=p_recv.at[c, step - 1],
            device_id=(other // 4, other % 4 * NZ + z, fs),
            device_id_type=MESH,
        )

    last = (8, 7)
    key_copy(0, 1).start()
    key_copy(1, 1).start()
    for c in range(CH):
        for way in range(2):
            row_copy(c, way, 1).start()
    for step in range(1, 9):
        for way in range(2):
            if step <= last[way]:
                key_arrival(way, step).wait_recv()
                if step < last[way]:
                    key_copy(way, step + 1).start()
        if step == 8:
            pieces = [keys[4 * q, 0:1, :] + keys[4 * q + 1, 0:1, :] + keys[4 * q + 2, 0:1, :] + keys[4 * q + 3, 0:1, :] for q in range(4)]
            row_key = jnp.concatenate(pieces, axis=1)
            place = lax.broadcasted_iota(jnp.int32, (256, 512), 0)
            column = lax.broadcasted_iota(jnp.int32, (256, 512), 1)
            wanted = (place & 224) + 2 * z + (place & 1) + 1
            same = ((place >> 1) & 15) == (column >> 5)
            chosen = jnp.where(same & (row_key == wanted), 1.0, 0.0).astype(jnp.bfloat16)
        for c in range(CH):
            for way in range(2):
                if step <= last[way]:
                    row_arrival(c, way, step).wait_recv()
                    if step < last[way]:
                        row_copy(c, way, step + 1).start()
            if step == 8:
                picked[c] = jnp.dot(chosen, rows[c], preferred_element_type=jnp.float32).astype(jnp.bfloat16)
                for hop in range(1, 8):
                    plane_copy(c, hop).start()
    for c in range(CH):
        own = pl.ds(pl.multiple_of(mine * 32, 32), 32)
        landed[c, own, :] = picked[c, own, :]
        for step in range(1, 8):
            plane_arrival(c, step).wait_recv()
        out_ref[:, c * CW : (c + 1) * CW] = landed[c]
    for way in range(2):
        for step in range(1, last[way] + 1):
            key_copy(way, step).wait_send()
            for c in range(CH):
                row_copy(c, way, step).wait_send()
    for c in range(CH):
        for step in range(1, 8):
            plane_copy(c, step).wait_send()


def deliver(merged, slots):
    width = merged.shape[1]
    return pl.pallas_call(
        deliver_kernel,
        out_shape=jax.ShapeDtypeStruct((256, width), jnp.bfloat16),
        in_specs=[pl.BlockSpec(memory_space=pltpu.VMEM)] * 2,
        out_specs=pl.BlockSpec(memory_space=pltpu.VMEM),
        scratch_shapes=[
            pltpu.VMEM((CH, 512, CW), jnp.bfloat16),
            pltpu.VMEM((NZ, 8, 128), jnp.int32),
            pltpu.VMEM((CH, 256, CW), jnp.bfloat16),
            pltpu.VMEM((CH, 256, CW), jnp.bfloat16),
            pltpu.SemaphoreType.DMA((CH, 2, 8)),
            pltpu.SemaphoreType.DMA((CH, 2, 8)),
            pltpu.SemaphoreType.DMA((2, 8)),
            pltpu.SemaphoreType.DMA((2, 8)),
            pltpu.SemaphoreType.DMA((CH, 7)),
            pltpu.SemaphoreType.DMA((CH, 7)),
        ],
        compiler_params=pltpu.CompilerParams(collective_id=0, has_side_effects=True),
    )(merged, slots)


def normalize(values_in, gain_row):
    widened = values_in.astype(jnp.float32)
    centered = widened - jnp.mean(widened, axis=1, keepdims=True)
    variance = jnp.mean(centered * centered, axis=1, keepdims=True)
    return (centered * lax.rsqrt(variance + epsilon) * gain_row).astype(jnp.bfloat16)


def attend(queries, keys_all, values_all, segs):
    factor = 1.0 / math.sqrt(HD)
    allowed = segs[:, None] == segs[None, :]
    pieces = []
    for head_index in range(queries.shape[1] // HD):
        first_col = head_index * HD
        last_col = first_col + HD
        scores = (
            lax.dot_general(
                queries[:, first_col:last_col],
                keys_all[:, first_col:last_col],
                (((1,), (1,)), ((), ())),
                preferred_element_type=jnp.float32,
            )
            * factor
        )
        masked = jnp.where(allowed, scores, -jnp.inf)
        highest = jnp.max(masked, axis=1, keepdims=True)
        weights = jnp.exp(masked - highest)
        totals = jnp.sum(weights, axis=1, keepdims=True)
        head_out = jnp.dot(
            weights.astype(jnp.bfloat16),
            values_all[:, first_col:last_col],
            preferred_element_type=jnp.float32,
        )
        pieces.append(head_out / totals)
    return jnp.concatenate(pieces, axis=1).astype(jnp.bfloat16)


def mix(left, right):
    return jnp.dot(left, right, preferred_element_type=jnp.float32)


def per_device(
    tokens, qkv_weight, out_weight, merge_weight, ln_gains, segments, merge_rows, owners
):
    bf = jnp.bfloat16
    xh = lax.axis_index("xh")
    fs = lax.axis_index("fsdp")
    z = lax.axis_index("yz") % NZ
    place = jnp.arange(1280, dtype=jnp.int32)
    natural = ((place % 80 // 10) * NZ + place // 80) * 10 + place % 10
    unmove = (natural[:, None] == jnp.arange(1280, dtype=jnp.int32)[None, :]).astype(bf)
    move = (natural[None, :] == jnp.arange(1280, dtype=jnp.int32)[:, None]).astype(bf)

    q_in = qkv_weight.reshape(3, 10, 2, 160).transpose(2, 1, 0, 3).reshape(2, 10, 480)
    q_in = jnp.pad(q_in, ((0, 0), (0, 6), (0, 32)))
    o_flat = out_weight.T
    o_in = jnp.where(fs % 2 == 0, jnp.pad(o_flat, ((0, 6), (0, 64))), jnp.pad(o_flat, ((0, 6), (64, 0))))
    m_in = jnp.pad(merge_weight, ((0, 6), (0, 0)))
    normed = mix(normalize(tokens, ln_gains[0]), move).astype(bf)
    tokens_moved = mix(tokens, move)
    gains_moved = jnp.sum(jnp.where(natural[:, None] == jnp.arange(1280)[None, :], ln_gains[1][None, :], 0.0), axis=1)
    seg_in = jnp.broadcast_to(segments, (8, 128))
    wq, wo, wm, normed_all, seg_all = gather_all(q_in, o_in, m_in, normed, seg_in)
    wq = wq.reshape(1280, 512)
    group_segs = seg_all[:, 0, :].reshape(2, 512)
    qkv = mix(normed_all.reshape(1024, 1280), wq).astype(bf)
    attended = []
    for g in range(2):
        mine = qkv[g * 512 : (g + 1) * 512]
        attended.append(attend(mine[:, 0:160], mine[:, 160:320], mine[:, 320:480], group_segs[g]))
    attended = jnp.concatenate(attended, axis=0).reshape(8, 128, 160)
    received = lax.all_to_all(attended, XG, split_axis=0, concat_axis=0, tiled=True)
    local = received.reshape(2, 4, 128, 160).transpose(2, 1, 0, 3).reshape(128, 1280)
    wo = wo.reshape(2, 1280, 640)
    update = lax.dot_general(local[:, :640], wo[0], (((1,), (1,)), ((), ())), preferred_element_type=jnp.float32)
    update = update + lax.dot_general(local[:, 640:], wo[1], (((1,), (1,)), ((), ())), preferred_element_type=jnp.float32)
    layer_out = (tokens_moved + update).astype(bf)
    merge_in = normalize(layer_out, gains_moved)
    order = merge_rows[0].reshape(32, 4).T.reshape(128)
    picker = (order[:, None] == jnp.arange(128, dtype=jnp.int32)[None, :]).astype(bf)
    stacked = mix(mix(picker, merge_in).astype(bf), unmove).astype(bf)
    blocks = stacked.reshape(4, 32, 2, 640).transpose(0, 2, 1, 3).reshape(8, 32, 640)
    inputs = lax.all_to_all(blocks, XG, split_axis=0, concat_axis=0, tiled=True).reshape(256, 640)
    partial = mix(inputs, wm.reshape(640, 1280)).astype(bf).reshape(8, 32, 1280)
    parts = lax.all_to_all(partial, XG, split_axis=0, concat_axis=0, tiled=True)
    merged = jnp.sum(parts.astype(jnp.float32), axis=0).astype(bf)
    targets = owners[:, 0]
    ranks = jnp.arange(32)
    position = jnp.sum((targets[:, None] == targets[None, :]) & (ranks[None, :] < ranks[:, None]), axis=1)
    slot_row = targets * 2 + position.astype(jnp.int32) + 1
    spread = jnp.where(jnp.arange(4)[:, None] == z % 4, slot_row[None, :], 0).reshape(1, 128)
    return deliver(merged, jnp.broadcast_to(spread, (8, 128)))


def solution(mesh):
    cut = Mesh(mesh.devices.reshape(2, 64, 4), ("xh", "yz", "fsdp"))
    every = ("xh", "yz", "fsdp")
    return jax.shard_map(
        per_device,
        mesh=cut,
        in_specs=(
            P(every, None),
            P(None, ("xh", "yz"), "fsdp"),
            P("fsdp", ("xh", "yz")),
            P(every, None),
            P(),
            P(("xh", "yz"), "fsdp"),
            P(every, None),
            P(every, None),
        ),
        out_specs=P(every, None),
        check_vma=False,
    )
```

```python
import math

import jax
import jax.numpy as jnp
from jax import lax
from jax.experimental import pallas as pl
from jax.experimental.pallas import tpu as pltpu
from jax.sharding import Mesh
from jax.sharding import PartitionSpec as P

HD = 80
NZ = 16
NY = 4
CH = 5
CW = 256
MESH = pl.DeviceIdType.MESH
epsilon = 1e-06


def coords():
    yz = lax.axis_index("yz")
    return lax.axis_index("xh"), yz // NZ, yz % NZ, lax.axis_index("fsdp")


def rows_of(place, n):
    return pl.ds(pl.multiple_of(place * n, n), n)


def center(values):
    middle = values - jnp.mean(values, axis=1, keepdims=True)
    variance = jnp.mean(middle * middle, axis=1, keepdims=True)
    return middle * lax.rsqrt(variance + epsilon)


def mix(left, right):
    return jnp.dot(left, right, preferred_element_type=jnp.float32)


def mix_t(left, right):
    return lax.dot_general(left, right, (((1,), (1,)), ((), ())), preferred_element_type=jnp.float32)


def block_kernel(
    tok_in, gain_in, q_in, o_in, m_in, seg_in, order_in, slot_in, out,
    wq, wo, wm, unmove, tok_t, normed_all, seg_all, q_box, o_box, m_box, slots,
    qkv, att_out, att_in, mi_out, mi_in, part_out, part_in, rows, picked, landed,
    q_send, q_recv, o_send, o_recv, m_send, m_recv, n_send, n_recv, g_send, g_recv,
    zq_send, zq_recv, zo_send, zo_recv, zm_send, zm_recv, s_send, s_recv,
    k_send, k_recv, a_send, a_recv, i_send, i_recv, r_send, r_recv, p_send, p_recv, z_send, z_recv,
):
    bf = jnp.bfloat16
    xh, y, z, fs = coords()
    core = fs % 2
    xlo = fs // 2
    mine = xh * 4 + y
    member = xh * 4 + fs
    up, down = (z + 1) % NZ, (z + NZ - 1) % NZ

    def dev(xh_, y_, z_, fs_):
        return (xh_, y_ * NZ + z_, fs_)

    barrier = pltpu.get_barrier_semaphore()
    for dx in range(2):
        for dy in range(4):
            for df in range(4):
                if dx or dy or df:
                    there = dev((xh + dx) % 2, (y + dy) % 4, z, (fs + df) % 4)
                    pl.semaphore_signal(barrier, inc=1, device_id=there, device_id_type=MESH)
    for dz in range(1, NZ):
        pl.semaphore_signal(barrier, inc=1, device_id=dev(xh, y, (z + dz) % NZ, fs), device_id_type=MESH)

    lane = lax.broadcasted_iota(jnp.int32, (128, 128), 1)
    for b in range(10):
        p = lax.broadcasted_iota(jnp.int32, (128, 128), 0) + b * 128
        pz = ((p >> 4) * 52429) >> 18
        rest = p - pz * 80
        tens = (rest * 52429) >> 19
        natural = (tens * NZ + pz) * 10 + (rest - tens * 10)
        for t in range(10):
            unmove[b * 128 : (b + 1) * 128, t * 128 : (t + 1) * 128] = jnp.where(
                natural == lane + t * 128, 1.0, 0.0
            ).astype(bf)
    normed = (center(tok_in[...].astype(jnp.float32)) * gain_in[0:1, :]).astype(bf)
    normed_all[member] = mix_t(normed, unmove[...]).astype(bf)
    seg_all[member] = seg_in[...]
    slots[mine] = slot_in[...]
    pl.semaphore_wait(barrier, 46)

    def copy(src, dst, ssem, rsem, where):
        return pltpu.make_async_remote_copy(
            src_ref=src, dst_ref=dst, send_sem=ssem, recv_sem=rsem, device_id=where, device_id_type=MESH
        )

    def q_copy(step):
        dx, dy = step // 4, step % 4
        oxh, oy = (xh + dx) % 2, (y + dy) % 4
        return copy(q_in.at[oxh], q_box.at[mine], q_send.at[step], q_recv.at[step], dev(oxh, oy, z, fs))

    def q_arrival(step):
        dx, dy = step // 4, step % 4
        oxh, oy = (xh + dx) % 2, (y + 4 - dy) % 4
        return copy(q_in.at[xh], q_box.at[oxh * 4 + oy], q_send.at[step], q_recv.at[step], dev(oxh, oy, z, fs))

    for step in range(1, 8):
        q_copy(step).start()
    q_box[mine] = q_in[xh]

    o_steps = [(dx, dl, dy) for dx in range(2) for dl in range(2) for dy in range(4)]

    def o_slot(c, d):
        return o_box.at[c, d]

    def o_copy(k):
        dx, dl, dy = o_steps[k]
        oxh, olo, oy = (xh + dx) % 2, (xlo + dl) % 2, (y + dy) % 4
        return copy(o_in, o_slot(core, mine), o_send.at[k], o_recv.at[core, k], dev(oxh, oy, z, olo * 2 + xlo))

    def o_arrival(c, k):
        dx, dl, dy = o_steps[k]
        oxh, oy = (xh + dx) % 2, (y + 4 - dy) % 4
        return copy(o_in, o_slot(c, oxh * 4 + oy), o_send.at[k], o_recv.at[c, k], dev(oxh, oy, z, core * 2 + c))

    def o_remote(k):
        dx, dl, dy = o_steps[k]
        if dx or dy:
            return None
        return (xlo + dl) % 2 * 2 + xlo != fs

    for k in range(16):
        cond = o_remote(k)
        if cond is None:
            o_copy(k).start()
        else:
            @pl.when(cond)
            def _():
                o_copy(k).start()

    @pl.when(xlo == core)
    def _():
        o_box[core, mine] = o_in[...]

    def m_copy(dy):
        return copy(m_in, m_box.at[fs], m_send.at[dy], m_recv.at[fs], dev(xh, (y + dy) % 4, z, y))

    def m_arrival(j):
        return copy(m_in, m_box.at[j], m_send.at[0], m_recv.at[j], dev(xh, fs, z, j))

    for dy in range(1, 4):
        m_copy(dy).start()

    @pl.when(fs != y)
    def _():
        m_copy(0).start()

    @pl.when(fs == y)
    def _():
        m_box[fs] = m_in[...]


    def k_pair(step, to):
        dx, dy = step // 4, step % 4
        oxh = (xh + dx) % 2
        oy = (y + dy) % 4 if to else (y + 4 - dy) % 4
        slot = mine if to else oxh * 4 + oy
        return copy(slot_in, slots.at[slot], k_send.at[step], k_recv.at[step], dev(oxh, oy, z, fs))

    def n_pair(step, to):
        dx, df = step // 4, step % 4
        oxh = (xh + dx) % 2
        ofs = (fs + df) % 4 if to else (fs + 4 - df) % 4
        slot = member if to else oxh * 4 + ofs
        there = dev(oxh, y, z, ofs)
        return (
            copy(normed_all.at[member], normed_all.at[slot], n_send.at[step], n_recv.at[step], there),
            copy(seg_in, seg_all.at[slot], g_send.at[step], g_recv.at[step], there),
        )

    for step in range(1, 8):
        for one in n_pair(step, True):
            one.start()
    for step in range(1, 8):
        k_pair(step, True).start()

    def ten(count, depth):
        place = lax.broadcasted_iota(jnp.int32, (count, depth), 0)
        column = lax.broadcasted_iota(jnp.int32, (count, depth), 1)
        tens = (place * 52429) >> 19
        return jnp.where(column == tens * 16 + (place - tens * 10), 1.0, 0.0).astype(bf)

    def settle(picker, block):
        return mix(picker, block).astype(bf)

    pick80 = ten(80, 128)
    for step in range(1, 8):
        q_arrival(step).wait_recv()
    wq[z] = settle(pick80, q_box[...].reshape(128, 512))

    last = (8, 7)

    def ring(buf, ssem, rsem, way, step, arriving):
        gone = step if arriving else step - 1
        src = (z + NZ - gone) % NZ if way == 0 else (z + gone) % NZ
        where = dev(xh, y, up if way == 0 else down, fs)
        return copy(buf.at[src], buf.at[src], ssem.at[way, step - 1], rsem.at[way, step - 1], where)

    q_ring = (wq, zq_send, zq_recv)
    o_ring = (wo.at[core], zo_send, zo_recv)
    m_ring = (wm, zm_send, zm_recv)
    sibling = dev(xh, y, z, xlo * 2 + 1 - core)

    def share(half, place, slot):
        return copy(wo.at[half, place], wo.at[half, place], s_send.at[slot], s_recv.at[slot], sibling)

    def begin(stream):
        for way in range(2):
            ring(*stream, way, 1, False).start()

    def serve(stream, step):
        for way in range(2):
            if step <= last[way]:
                ring(*stream, way, step, True).wait_recv()
                if step < last[way]:
                    ring(*stream, way, step + 1, False).start()
                if stream is o_ring:
                    place = (z + NZ - step) % NZ if way == 0 else (z + step) % NZ
                    share(core, place, step + 8 * way).start()

    begin(q_ring)
    for c in range(2):
        for k in range(16):
            dx, dl, dy = o_steps[k]
            here = (core + dl) % 2 == xlo
            cond = here if dx or dy else here & (core * 2 + c != fs)

            @pl.when(cond)
            def _():
                o_arrival(c, k).wait_recv()
    left = o_box[0].reshape(128, 384)
    right = o_box[1].reshape(128, 384)
    wo[core, z, :, 0:256] = settle(pick80, left[:, 0:256])
    wo[core, z, :, 256:384] = settle(pick80, left[:, 256:384] + right[:, 0:128])
    wo[core, z, :, 384:640] = settle(pick80, right[:, 128:384])
    begin(o_ring)
    share(core, z, 0).start()
    for j in range(4):
        @pl.when((j != fs) | (y != fs))
        def _():
            m_arrival(j).wait_recv()
    wm[z] = settle(ten(40, 64), m_box[...].reshape(64, 1280))
    tok_t[...] = mix_t(unmove[...], tok_in[...]).astype(bf)

    for step in range(1, 9):
        serve(q_ring, step)
        if step % 2 == 0:
            serve(o_ring, step // 2)
        if step == 6:
            begin(m_ring)
    for step in range(1, 8):
        for one in n_pair(step, False):
            one.wait_recv()

    factor = 1.0 / math.sqrt(HD)

    def a_copy(step, to):
        dx, df = step // 4, step % 4
        oxh = (xh + dx) % 2
        ofs = (fs + df) % 4 if to else (fs + 4 - df) % 4
        head = fs * 2 + xh if to else ofs * 2 + oxh
        return copy(
            att_out.at[oxh * 4 + ofs], att_in.at[rows_of(head, 160), :], a_send.at[step], a_recv.at[step], dev(oxh, y, z, ofs)
        )

    def project(g):
        block = normed_all[g * 4 : (g + 1) * 4].reshape(512, 1280)
        qkv[g] = mix(block, wq[...].reshape(1280, 512)).astype(bf)

    def attend(g):
        across = jnp.concatenate([seg_all[g * 4 + b, 0:1, :] for b in range(4)], axis=1)
        downs = []
        for b in range(4):
            one = jnp.broadcast_to(seg_all[g * 4 + b, 0:1, :].astype(jnp.float32), (128, 128)).T
            downs.append(jnp.concatenate([one] * 4, axis=1))
        allowed = jnp.concatenate(downs, axis=0) == across.astype(jnp.float32)
        for h in range(2):
            query = qkv[g, :, h * HD : h * HD + HD]
            key = qkv[g, :, 160 + h * HD : 160 + h * HD + HD]
            value = qkv[g, :, 320 + h * HD : 320 + h * HD + HD]
            scores = jnp.where(allowed, mix_t(key, query) * factor, -jnp.inf)
            weights = jnp.exp(scores - jnp.max(scores, axis=0, keepdims=True))
            totals = jnp.sum(weights, axis=0, keepdims=True)
            value_t = value.astype(jnp.float32).T.astype(bf)
            head_out = (mix(value_t, weights.astype(bf)) / totals).astype(bf)
            for b in range(4):
                att_out[g * 4 + b, h * HD : h * HD + HD, :] = head_out[:, b * 128 : (b + 1) * 128]

    project(0)
    serve(o_ring, 5)
    attend(0)
    serve(m_ring, 1)
    project(1)
    serve(o_ring, 6)
    attend(1)
    att_in[rows_of(fs * 2 + xh, 160), :] = att_out[member]
    for step in range(1, 8):
        a_copy(step, True).start()
    serve(m_ring, 2)
    serve(o_ring, 7)
    serve(m_ring, 3)
    serve(o_ring, 8)
    for step in range(1, 8):
        a_copy(step, False).wait_recv()
    share(1 - core, z, 0).wait_recv()
    for way in range(2):
        for step in range(1, last[way] + 1):
            place = (z + NZ - step) % NZ if way == 0 else (z + step) % NZ
            share(1 - core, place, step + 8 * way).wait_recv()

    update = mix(wo[0].reshape(1280, 640), att_in[0:640, :]) + mix(wo[1].reshape(1280, 640), att_in[640:1280, :])
    layer_t = (tok_t[...].astype(jnp.float32) + update).astype(bf)
    picker = jnp.where(order_in[...] == lane, 1.0, 0.0).astype(bf)
    chosen = mix_t(picker, layer_t).astype(bf)
    merge_in = (center(mix(chosen, unmove[...])) * gain_in[1:2, :]).astype(bf)
    for b in range(8):
        mi_out[b] = merge_in[b // 2 * 32 : b // 2 * 32 + 32, b % 2 * 640 : b % 2 * 640 + 640]

    def i_copy(step, to):
        dx, df = step // 4, step % 4
        oxh = (xh + dx) % 2
        ofs = (fs + df) % 4 if to else (fs + 4 - df) % 4
        other = oxh * 4 + ofs
        slot = member if to else other
        return copy(mi_out.at[other], mi_in.at[slot], i_send.at[step], i_recv.at[step], dev(oxh, y, z, ofs))

    for step in range(1, 8):
        i_copy(step, True).start()
    mi_in[member] = mi_out[member]
    for step in range(4, 9):
        serve(m_ring, step)
    for step in range(1, 8):
        i_copy(step, False).wait_recv()

    def r_copy(c, step, to):
        dx, df = step // 4, step % 4
        oxh = (xh + dx) % 2
        ofs = (fs + df) % 4 if to else (fs + 4 - df) % 4
        other = oxh * 4 + ofs
        slot = member if to else other
        return copy(
            part_out.at[c, other], part_in.at[c, slot], r_send.at[c, step], r_recv.at[c, step], dev(oxh, y, z, ofs)
        )

    inputs = mi_in[...].reshape(256, 640)
    for c in range(CH):
        part = mix(inputs, wm[:, :, c * CW : (c + 1) * CW].reshape(640, CW)).astype(bf)
        part_out[c] = part.reshape(8, 32, CW)
        for step in range(1, 8):
            r_copy(c, step, True).start()
        part_in[c, member] = part_out[c, member]

    def p_copy(c, step, to):
        dx, dy = step // 4, step % 4
        oxh = (xh + dx) % 2
        oy = (y + dy) % 4 if to else (y + 4 - dy) % 4
        slot = mine if to else oxh * 4 + oy
        return copy(
            rows.at[c, mine], rows.at[c, slot], p_send.at[c, step], p_recv.at[c, step], dev(oxh, oy, z, fs)
        )

    for c in range(CH):
        for step in range(1, 8):
            r_copy(c, step, False).wait_recv()
        rows[c, mine] = jnp.sum(part_in[c].astype(jnp.float32), axis=0).astype(bf)
        for step in range(1, 8):
            p_copy(c, step, True).start()

    def z_copy(c, step, to):
        other = (z + step) % NZ if to else (z + NZ - step) % NZ
        slot = z if to else other
        return copy(
            picked.at[c, rows_of(other, 16), :], landed.at[c, rows_of(slot, 16), :],
            z_send.at[c, step], z_recv.at[c, step], dev(xh, y, other, fs),
        )

    for step in range(1, 8):
        k_pair(step, False).wait_recv()
    row_key = jnp.concatenate(
        [slots[4 * q, 0:1, :] + slots[4 * q + 1, 0:1, :] + slots[4 * q + 2, 0:1, :] + slots[4 * q + 3, 0:1, :] for q in range(2)],
        axis=1,
    )
    place = lax.broadcasted_iota(jnp.int32, (256, 256), 0)
    column = lax.broadcasted_iota(jnp.int32, (256, 256), 1)
    wanted = (mine * NZ + (place >> 4)) * 2 + (place & 1) + 1
    select = jnp.where((((place >> 1) & 7) == (column >> 5)) & (row_key == wanted), 1.0, 0.0).astype(bf)
    for c in range(CH):
        for step in range(1, 8):
            p_copy(c, step, False).wait_recv()
        picked[c] = mix(select, rows[c].reshape(256, CW)).astype(bf)
        for step in range(1, NZ):
            z_copy(c, step, True).start()
    turned = (((place >> 1) & 15) << 4) + ((place >> 5) << 1) + (place & 1)
    turn = jnp.where(turned == column, 1.0, 0.0).astype(bf)
    for c in range(CH):
        own = rows_of(z, 16)
        landed[c, own, :] = picked[c, own, :]
        for step in range(1, NZ):
            z_copy(c, step, False).wait_recv()
        out[:, c * CW : (c + 1) * CW] = mix(turn, landed[c]).astype(bf)

    for step in range(1, 8):
        q_copy(step).wait_send()
        for one in n_pair(step, True):
            one.wait_send()
        k_pair(step, True).wait_send()
        a_copy(step, True).wait_send()
        i_copy(step, True).wait_send()
        for c in range(CH):
            r_copy(c, step, True).wait_send()
            p_copy(c, step, True).wait_send()
    for step in range(1, NZ):
        for c in range(CH):
            z_copy(c, step, True).wait_send()
    for k in range(16):
        cond = o_remote(k)
        if cond is None:
            o_copy(k).wait_send()
        else:
            @pl.when(cond)
            def _():
                o_copy(k).wait_send()
    for dy in range(1, 4):
        m_copy(dy).wait_send()

    @pl.when(fs != y)
    def _():
        m_copy(0).wait_send()

    share(core, z, 0).wait_send()
    for way in range(2):
        for step in range(1, last[way] + 1):
            for stream in (q_ring, o_ring, m_ring):
                ring(*stream, way, step, False).wait_send()
            place_ = (z + NZ - step) % NZ if way == 0 else (z + step) % NZ
            share(core, place_, step + 8 * way).wait_send()


def block(*operands):
    bf = jnp.bfloat16
    dma = pltpu.SemaphoreType.DMA
    vm = pltpu.VMEM
    return pl.pallas_call(
        block_kernel,
        out_shape=jax.ShapeDtypeStruct((256, 1280), bf),
        in_specs=[pl.BlockSpec(memory_space=pltpu.VMEM)] * 8,
        out_specs=pl.BlockSpec(memory_space=pltpu.VMEM),
        scratch_shapes=[
            vm((NZ, 80, 512), bf), vm((2, NZ, 80, 640), bf), vm((NZ, 40, 1280), bf), vm((1280, 1280), bf),
            vm((1280, 128), bf), vm((8, 128, 1280), bf), vm((8, 8, 128), jnp.int32),
            vm((8, 16, 512), bf), vm((2, 8, 16, 384), bf), vm((4, 16, 1280), bf), vm((8, 8, 128), jnp.int32),
            vm((2, 512, 512), bf), vm((8, 160, 128), bf), vm((1280, 128), bf), vm((8, 32, 640), bf), vm((8, 32, 640), bf),
            vm((CH, 8, 32, CW), bf), vm((CH, 8, 32, CW), bf), vm((CH, 8, 32, CW), bf), vm((CH, 256, CW), bf), vm((CH, 256, CW), bf),
            dma((8,)), dma((8,)), dma((16,)), dma((2, 16)), dma((4,)), dma((4,)),
            dma((8,)), dma((8,)), dma((8,)), dma((8,)),
            dma((2, 8)), dma((2, 8)), dma((2, 8)), dma((2, 8)), dma((2, 8)), dma((2, 8)),
            dma((17,)), dma((17,)),
            dma((8,)), dma((8,)), dma((8,)), dma((8,)), dma((8,)), dma((8,)),
            dma((CH, 8)), dma((CH, 8)), dma((CH, 8)), dma((CH, 8)), dma((CH, NZ)), dma((CH, NZ)),
        ],
        compiler_params=pltpu.CompilerParams(collective_id=1, has_side_effects=True, vmem_limit_bytes=60 << 20),
    )(*operands)


def per_device(
    tokens, qkv_weight, out_weight, merge_weight, ln_gains, segments, merge_rows, owners
):
    fs = lax.axis_index("fsdp")
    y = lax.axis_index("yz") // NZ
    q_in = qkv_weight.reshape(3, 10, 2, 160).transpose(2, 1, 0, 3).reshape(2, 10, 480)
    q_in = jnp.pad(q_in, ((0, 0), (0, 6), (0, 32)))
    o_flat = out_weight.T
    o_in = jnp.where(fs % 2 == 0, jnp.pad(o_flat, ((0, 6), (0, 64))), jnp.pad(o_flat, ((0, 6), (64, 0))))
    m_in = jnp.pad(merge_weight, ((0, 6), (0, 0)))
    seg_in = jnp.broadcast_to(segments, (8, 128))
    order = merge_rows[0].reshape(32, 4).T.reshape(128, 1)
    order_in = jnp.broadcast_to(order, (128, 128))
    targets = owners[:, 0]
    ranks = jnp.arange(32)
    earlier = (targets[:, None] == targets[None, :]) & (ranks[None, :] < ranks[:, None])
    slot_row = targets * 2 + jnp.sum(earlier.astype(jnp.int32), axis=1) + 1
    spread = jnp.where(jnp.arange(4)[:, None] == y, slot_row[None, :], 0).reshape(1, 128)
    slot_in = jnp.broadcast_to(spread, (8, 128))
    return block(tokens, ln_gains, q_in, o_in, m_in, seg_in, order_in, slot_in)


def solution(mesh):
    cut = Mesh(mesh.devices.reshape(2, 64, 4), ("xh", "yz", "fsdp"))
    every = ("xh", "yz", "fsdp")
    return jax.shard_map(
        per_device,
        mesh=cut,
        in_specs=(
            P(every, None),
            P(None, ("xh", "yz"), "fsdp"),
            P("fsdp", ("xh", "yz")),
            P(every, None),
            P(),
            P(("xh", "yz"), "fsdp"),
            P(every, None),
            P(every, None),
        ),
        out_specs=P(every, None),
        check_vma=False,
    )
```

```python
import math

import jax
import jax.numpy as jnp
from jax import lax
from jax.experimental import pallas as pl
from jax.experimental.pallas import tpu as pltpu
from jax.sharding import Mesh
from jax.sharding import PartitionSpec as P

HD = 80
NZ = 16
NY = 4
CH = 5
CW = 256
MESH = pl.DeviceIdType.MESH
epsilon = 1e-06


def coords():
    yz = lax.axis_index("yz")
    return lax.axis_index("xh"), yz // NZ, yz % NZ, lax.axis_index("fsdp")


def rows_of(place, n):
    return pl.ds(pl.multiple_of(place * n, n), n)


def center(values):
    middle = values - jnp.mean(values, axis=1, keepdims=True)
    variance = jnp.mean(middle * middle, axis=1, keepdims=True)
    return middle * lax.rsqrt(variance + epsilon)


def mix(left, right):
    return jnp.dot(left, right, preferred_element_type=jnp.float32)


def mix_t(left, right):
    return lax.dot_general(left, right, (((1,), (1,)), ((), ())), preferred_element_type=jnp.float32)


def block_kernel(
    tok_in, gain_in, q_in, o_in, m_in, seg_in, order_in, slot_in, out,
    wq, wo, wm, unmove, tok_t, normed_all, seg_all, q_box, o_box, m_box, slots,
    qkv, att_out, att_in, mi_out, mi_in, part_out, part_in, rows, picked, landed,
    c_send, c_recv, y_send, y_recv, e_send, e_recv,
    q_send, q_recv, o_send, o_recv, m_send, m_recv, n_send, n_recv, g_send, g_recv,
    s_send, s_recv, a_send, a_recv, i_send, i_recv, r_send, r_recv, p_send, p_recv,
):
    bf = jnp.bfloat16
    xh, y, z, fs = coords()
    core = fs % 2
    xlo = fs // 2
    mine = xh * 4 + y
    member = xh * 4 + fs
    up, down = (z + 1) % NZ, (z + NZ - 1) % NZ

    def dev(xh_, y_, z_, fs_):
        return (xh_, y_ * NZ + z_, fs_)

    barrier = pltpu.get_barrier_semaphore()
    for dx in range(2):
        for dy in range(4):
            for df in range(4):
                if dx or dy or df:
                    there = dev((xh + dx) % 2, (y + dy) % 4, z, (fs + df) % 4)
                    pl.semaphore_signal(barrier, inc=1, device_id=there, device_id_type=MESH)
    for peer in (up, down):
        pl.semaphore_signal(barrier, inc=1, device_id=dev(xh, y, peer, fs), device_id_type=MESH)

    lane = lax.broadcasted_iota(jnp.int32, (128, 128), 1)
    for b in range(10):
        p = lax.broadcasted_iota(jnp.int32, (128, 128), 0) + b * 128
        pz = ((p >> 4) * 52429) >> 18
        rest = p - pz * 80
        tens = (rest * 52429) >> 19
        natural = (tens * NZ + pz) * 10 + (rest - tens * 10)
        for t in range(10):
            unmove[b * 128 : (b + 1) * 128, t * 128 : (t + 1) * 128] = jnp.where(
                natural == lane + t * 128, 1.0, 0.0
            ).astype(bf)
    normed = (center(tok_in[...].astype(jnp.float32)) * gain_in[0:1, :]).astype(bf)
    normed_all[member] = mix_t(normed, unmove[...]).astype(bf)
    seg_all[member] = seg_in[...]
    slots[z] = slot_in[...]
    pl.semaphore_wait(barrier, 33)

    def copy(src, dst, ssem, rsem, where):
        return pltpu.make_async_remote_copy(
            src_ref=src, dst_ref=dst, send_sem=ssem, recv_sem=rsem, device_id=where, device_id_type=MESH
        )

    def q_copy(step):
        dx, dy = step // 4, step % 4
        oxh, oy = (xh + dx) % 2, (y + dy) % 4
        return copy(q_in.at[oxh], q_box.at[mine], q_send.at[step], q_recv.at[step], dev(oxh, oy, z, fs))

    def q_arrival(step):
        dx, dy = step // 4, step % 4
        oxh, oy = (xh + dx) % 2, (y + 4 - dy) % 4
        return copy(q_in.at[xh], q_box.at[oxh * 4 + oy], q_send.at[step], q_recv.at[step], dev(oxh, oy, z, fs))

    for step in range(1, 8):
        q_copy(step).start()
    q_box[mine] = q_in[xh]

    o_steps = [(dx, dl, dy) for dx in range(2) for dl in range(2) for dy in range(4)]

    def o_slot(c, d):
        return o_box.at[c, d]

    def o_copy(k):
        dx, dl, dy = o_steps[k]
        oxh, olo, oy = (xh + dx) % 2, (xlo + dl) % 2, (y + dy) % 4
        return copy(o_in, o_slot(core, mine), o_send.at[k], o_recv.at[core, k], dev(oxh, oy, z, olo * 2 + xlo))

    def o_arrival(c, k):
        dx, dl, dy = o_steps[k]
        oxh, oy = (xh + dx) % 2, (y + 4 - dy) % 4
        return copy(o_in, o_slot(c, oxh * 4 + oy), o_send.at[k], o_recv.at[c, k], dev(oxh, oy, z, core * 2 + c))

    def o_remote(k):
        dx, dl, dy = o_steps[k]
        if dx or dy:
            return None
        return (xlo + dl) % 2 * 2 + xlo != fs

    for k in range(16):
        cond = o_remote(k)
        if cond is None:
            o_copy(k).start()
        else:
            @pl.when(cond)
            def _():
                o_copy(k).start()

    @pl.when(xlo == core)
    def _():
        o_box[core, mine] = o_in[...]

    def m_copy(dy):
        return copy(m_in, m_box.at[fs], m_send.at[dy], m_recv.at[fs], dev(xh, (y + dy) % 4, z, y))

    def m_arrival(j):
        return copy(m_in, m_box.at[j], m_send.at[0], m_recv.at[j], dev(xh, fs, z, j))

    for dy in range(1, 4):
        m_copy(dy).start()

    @pl.when(fs != y)
    def _():
        m_copy(0).start()

    @pl.when(fs == y)
    def _():
        m_box[fs] = m_in[...]


    sibling = dev(xh, y, z, xlo * 2 + 1 - core)
    spot = xh * 2 + xlo

    def n_copy(dx, to):
        other = (spot + dx) % 4 if to else (spot + 4 - dx) % 4
        oxh, ofs = other // 2, other % 2 * 2 + core
        slot = member if to else oxh * 4 + ofs
        return copy(normed_all.at[member], normed_all.at[slot], n_send.at[dx], n_recv.at[dx], dev(oxh, y, z, ofs))

    def n_share(dx, to):
        other = (spot + 4 - dx) % 4
        slot = other // 2 * 4 + other % 2 * 2 + (core if to else 1 - core)
        return copy(normed_all.at[slot], normed_all.at[slot], n_send.at[4 + dx], n_recv.at[4 + dx], sibling)

    def g_copy(step, to):
        dx, df = step // 4, step % 4
        oxh = (xh + dx) % 2
        ofs = (fs + df) % 4 if to else (fs + 4 - df) % 4
        slot = member if to else oxh * 4 + ofs
        return copy(seg_in, seg_all.at[slot], g_send.at[step], g_recv.at[step], dev(oxh, y, z, ofs))

    for dx in (1, 3, 2):
        n_copy(dx, True).start()
    n_share(0, True).start()
    for step in range(1, 8):
        g_copy(step, True).start()

    def ten(count, depth):
        place = lax.broadcasted_iota(jnp.int32, (count, depth), 0)
        column = lax.broadcasted_iota(jnp.int32, (count, depth), 1)
        tens = (place * 52429) >> 19
        return jnp.where(column == tens * 16 + (place - tens * 10), 1.0, 0.0).astype(bf)

    def settle(picker, block):
        return mix(picker, block).astype(bf)

    pick80 = ten(80, 128)
    for step in range(1, 8):
        q_arrival(step).wait_recv()
    wq[z] = settle(pick80, q_box[...].reshape(128, 512))

    last = (8, 7)
    o_tile = y + y // 2
    o_part = pl.ds(pl.multiple_of(o_tile * 128, 128), 128)
    m_part = pl.ds(pl.multiple_of(y * 256, 256), 256)
    views = (
        lambda src: wq.at[src],
        lambda src: wo.at[core, src, :, o_part],
        lambda src: wo.at[core, src, :, pl.ds(256, 128)],
        lambda src: wm.at[src, :, m_part],
        lambda src: wm.at[src, :, pl.ds(1024, 256)],
        lambda src: slots.at[src],
    )

    def block_at(way, gone):
        return (z + NZ - gone) % NZ if way == 0 else (z + gone) % NZ

    def ring(k, way, step, arriving):
        view = views[k](block_at(way, step if arriving else step - 1))
        where = dev(xh, y, up if way == 0 else down, fs)
        return copy(view, view, c_send.at[k, way, step - 1], c_recv.at[k, way, step - 1], where)

    def begin(k):
        for way in range(2):
            ring(k, way, 1, False).start()

    def share(half, place, slot):
        return copy(wo.at[half, place], wo.at[half, place], s_send.at[slot], s_recv.at[slot], sibling)

    def o_along(place, slot, dy, to):
        oy = (y + dy) % 4 if to else (y + 4 - dy) % 4
        part = o_part if to else pl.ds(pl.multiple_of((oy + oy // 2) * 128, 128), 128)
        view = wo.at[core, place, :, part]
        return copy(view, view, y_send.at[slot, dy - 1], y_recv.at[slot, dy - 1], dev(xh, oy, z, fs))

    def m_along(place, slot, dy, to):
        oy = (y + dy) % 4 if to else (y + 4 - dy) % 4
        part = m_part if to else pl.ds(pl.multiple_of(oy * 256, 256), 256)
        view = wm.at[place, :, part]
        return copy(view, view, y_send.at[slot, dy + 2], y_recv.at[slot, dy + 2], dev(xh, oy, z, fs))

    def places(step):
        if step == 0:
            return [(z, 0)]
        return [(block_at(way, step), step + 8 * way) for way in range(2) if step <= last[way]]

    def serve(step):
        for k in (0, 1, 3, 2, 4, 5):
            for way in range(2):
                if step <= last[way]:
                    ring(k, way, step, True).wait_recv()
                    if step < last[way]:
                        ring(k, way, step + 1, False).start()

    def spread_out(step):
        for place, slot in places(step):
            for dy in (1, 3, 2):
                o_along(place, slot, dy, True).start()
        for place, slot in places(step):
            for dy in (1, 3, 2):
                m_along(place, slot, dy, True).start()

    def pass_on(step):
        for place, slot in places(step):
            for dy in range(1, 4):
                o_along(place, slot, dy, False).wait_recv()
            share(core, place, slot).start()

    begin(0)
    begin(5)
    for c in range(2):
        for k in range(16):
            dx, dl, dy = o_steps[k]
            here = (core + dl) % 2 == xlo
            cond = here if dx or dy else here & (core * 2 + c != fs)

            @pl.when(cond)
            def _():
                o_arrival(c, k).wait_recv()
    wo[core, z, :, 256:384] = settle(pick80, (o_box[0, :, :, 256:384] + o_box[1, :, :, 0:128]).reshape(128, 128))
    from_lane = pl.ds(pl.multiple_of((y % 2 + y // 2) * 128, 128), 128)
    wo[core, z, :, o_part] = settle(pick80, o_box[y // 2, :, :, from_lane].reshape(128, 128))
    begin(1)
    begin(2)
    for j in range(4):
        @pl.when((j != fs) | (y != fs))
        def _():
            m_arrival(j).wait_recv()
    pick40 = ten(40, 64)
    wm[z, :, m_part] = settle(pick40, m_box[:, :, m_part].reshape(64, 256))
    wm[z, :, 1024:1280] = settle(pick40, m_box[:, :, 1024:1280].reshape(64, 256))
    begin(3)
    begin(4)
    spread_out(0)
    tok_t[...] = mix_t(unmove[...], tok_in[...]).astype(bf)

    for step in range(1, 9):
        serve(step)
        spread_out(step)
        pass_on(step - 1)
        if step == 4:
            for dx in (1, 3):
                n_copy(dx, False).wait_recv()
                n_share(dx, True).start()
        if step == 6:
            n_copy(2, False).wait_recv()
            n_share(2, True).start()
    for dx in range(4):
        n_share(dx, False).wait_recv()
    for step in range(1, 8):
        g_copy(step, False).wait_recv()

    factor = 1.0 / math.sqrt(HD)

    def a_copy(step, to):
        dx, df = step // 4, step % 4
        oxh = (xh + dx) % 2
        ofs = (fs + df) % 4 if to else (fs + 4 - df) % 4
        head = fs * 2 + xh if to else ofs * 2 + oxh
        return copy(
            att_out.at[oxh * 4 + ofs], att_in.at[rows_of(head, 160), :], a_send.at[step], a_recv.at[step], dev(oxh, y, z, ofs)
        )

    def project(g):
        block = normed_all[g * 4 : (g + 1) * 4].reshape(512, 1280)
        qkv[g] = mix(block, wq[...].reshape(1280, 512)).astype(bf)

    def attend(g):
        across = jnp.concatenate([seg_all[g * 4 + b, 0:1, :] for b in range(4)], axis=1)
        downs = []
        for b in range(4):
            one = jnp.broadcast_to(seg_all[g * 4 + b, 0:1, :].astype(jnp.float32), (128, 128)).T
            downs.append(jnp.concatenate([one] * 4, axis=1))
        allowed = jnp.concatenate(downs, axis=0) == across.astype(jnp.float32)
        for h in range(2):
            query = qkv[g, :, h * HD : h * HD + HD]
            key = qkv[g, :, 160 + h * HD : 160 + h * HD + HD]
            value = qkv[g, :, 320 + h * HD : 320 + h * HD + HD]
            scores = jnp.where(allowed, mix_t(key, query) * factor, -jnp.inf)
            weights = jnp.exp(scores - jnp.max(scores, axis=0, keepdims=True))
            totals = jnp.sum(weights, axis=0, keepdims=True)
            value_t = value.astype(jnp.float32).T.astype(bf)
            head_out = (mix(value_t, weights.astype(bf)) / totals).astype(bf)
            for b in range(4):
                att_out[g * 4 + b, h * HD : h * HD + HD, :] = head_out[:, b * 128 : (b + 1) * 128]

    project(0)
    attend(0)
    project(1)
    attend(1)
    att_in[rows_of(fs * 2 + xh, 160), :] = att_out[member]
    for step in range(1, 8):
        a_copy(step, True).start()
    pass_on(8)
    for step in range(1, 8):
        a_copy(step, False).wait_recv()
    for step in range(9):
        for place, slot in places(step):
            share(1 - core, place, slot).wait_recv()

    update = mix(wo[0].reshape(1280, 640), att_in[0:640, :]) + mix(wo[1].reshape(1280, 640), att_in[640:1280, :])
    layer_t = (tok_t[...].astype(jnp.float32) + update).astype(bf)
    picker = jnp.where(order_in[...] == lane, 1.0, 0.0).astype(bf)
    chosen = mix_t(picker, layer_t).astype(bf)
    merge_in = (center(mix(chosen, unmove[...])) * gain_in[1:2, :]).astype(bf)
    for b in range(8):
        mi_out[b] = merge_in[b // 2 * 32 : b // 2 * 32 + 32, b % 2 * 640 : b % 2 * 640 + 640]

    def i_copy(step, to):
        dx, df = step // 4, step % 4
        oxh = (xh + dx) % 2
        ofs = (fs + df) % 4 if to else (fs + 4 - df) % 4
        other = oxh * 4 + ofs
        slot = member if to else other
        return copy(mi_out.at[other], mi_in.at[slot], i_send.at[step], i_recv.at[step], dev(oxh, y, z, ofs))

    for step in range(1, 8):
        i_copy(step, True).start()
    mi_in[member] = mi_out[member]
    for step in range(9):
        for place, slot in places(step):
            for dy in range(1, 4):
                m_along(place, slot, dy, False).wait_recv()
    for step in range(1, 8):
        i_copy(step, False).wait_recv()

    def r_copy(c, step, to):
        dx, df = step // 4, step % 4
        oxh = (xh + dx) % 2
        ofs = (fs + df) % 4 if to else (fs + 4 - df) % 4
        other = oxh * 4 + ofs
        slot = member if to else other
        return copy(
            part_out.at[c, other], part_in.at[c, slot], r_send.at[c, step], r_recv.at[c, step], dev(oxh, y, z, ofs)
        )

    inputs = mi_in[...].reshape(256, 640)
    for c in range(CH):
        part = mix(inputs, wm[:, :, c * CW : (c + 1) * CW].reshape(640, CW)).astype(bf)
        part_out[c] = part.reshape(8, 32, CW)
        for step in range(1, 8):
            r_copy(c, step, True).start()
        part_in[c, member] = part_out[c, member]

    def e_copy(c, way, step, arriving):
        view = rows.at[c, rows_of(block_at(way, step if arriving else step - 1), 32), :]
        where = dev(xh, y, up if way == 0 else down, fs)
        return copy(view, view, e_send.at[c, way, step - 1], e_recv.at[c, way, step - 1], where)

    for c in range(CH):
        for step in range(1, 8):
            r_copy(c, step, False).wait_recv()
        rows[c, rows_of(z, 32), :] = jnp.sum(part_in[c].astype(jnp.float32), axis=0).astype(bf)
        for way in range(2):
            e_copy(c, way, 1, False).start()

    def p_copy(c, step, to):
        dx, dy = step // 4, step % 4
        oxh = (xh + dx) % 2
        oy = (y + dy) % 4 if to else (y + 4 - dy) % 4
        other = oxh * 4 + oy
        slot = mine if to else other
        return copy(
            picked.at[c, rows_of(other, 32), :], landed.at[c, rows_of(slot, 32), :],
            p_send.at[c, step], p_recv.at[c, step], dev(oxh, oy, z, fs),
        )

    row_key = jnp.concatenate(
        [slots[4 * q, 0:1, :] + slots[4 * q + 1, 0:1, :] + slots[4 * q + 2, 0:1, :] + slots[4 * q + 3, 0:1, :] for q in range(4)],
        axis=1,
    )
    place = lax.broadcasted_iota(jnp.int32, (256, 512), 0)
    column = lax.broadcasted_iota(jnp.int32, (256, 512), 1)
    wanted = (place & 224) + 2 * z + (place & 1) + 1
    select = jnp.where((((place >> 1) & 15) == (column >> 5)) & (row_key == wanted), 1.0, 0.0).astype(bf)
    for step in range(1, 9):
        for c in range(CH):
            for way in range(2):
                if step <= last[way]:
                    e_copy(c, way, step, True).wait_recv()
                    if step < last[way]:
                        e_copy(c, way, step + 1, False).start()
            if step == 8:
                picked[c] = mix(select, rows[c]).astype(bf)
                for hop in range(1, 8):
                    p_copy(c, hop, True).start()
    own = rows_of(mine, 32)
    for c in range(CH):
        landed[c, own, :] = picked[c, own, :]
        for step in range(1, 8):
            p_copy(c, step, False).wait_recv()
        out[:, c * CW : (c + 1) * CW] = landed[c]

    for step in range(1, 8):
        q_copy(step).wait_send()
        g_copy(step, True).wait_send()
        a_copy(step, True).wait_send()
        i_copy(step, True).wait_send()
        for c in range(CH):
            r_copy(c, step, True).wait_send()
            p_copy(c, step, True).wait_send()
    for dx in range(4):
        n_share(dx, True).wait_send()
        if dx:
            n_copy(dx, True).wait_send()
    for k in range(16):
        cond = o_remote(k)
        if cond is None:
            o_copy(k).wait_send()
        else:
            @pl.when(cond)
            def _():
                o_copy(k).wait_send()
    for dy in range(1, 4):
        m_copy(dy).wait_send()

    @pl.when(fs != y)
    def _():
        m_copy(0).wait_send()

    for way in range(2):
        for step in range(1, last[way] + 1):
            for k in range(6):
                ring(k, way, step, False).wait_send()
            for c in range(CH):
                e_copy(c, way, step, False).wait_send()
    for step in range(9):
        for place_, slot in places(step):
            share(core, place_, slot).wait_send()
            for dy in range(1, 4):
                o_along(place_, slot, dy, True).wait_send()
                m_along(place_, slot, dy, True).wait_send()


def block(*operands):
    bf = jnp.bfloat16
    dma = pltpu.SemaphoreType.DMA
    vm = pltpu.VMEM
    return pl.pallas_call(
        block_kernel,
        out_shape=jax.ShapeDtypeStruct((256, 1280), bf),
        in_specs=[pl.BlockSpec(memory_space=pltpu.VMEM)] * 8,
        out_specs=pl.BlockSpec(memory_space=pltpu.VMEM),
        scratch_shapes=[
            vm((NZ, 80, 512), bf), vm((2, NZ, 80, 640), bf), vm((NZ, 40, 1280), bf), vm((1280, 1280), bf),
            vm((1280, 128), bf), vm((8, 128, 1280), bf), vm((8, 8, 128), jnp.int32),
            vm((8, 16, 512), bf), vm((2, 8, 16, 384), bf), vm((4, 16, 1280), bf), vm((NZ, 8, 128), jnp.int32),
            vm((2, 512, 512), bf), vm((8, 160, 128), bf), vm((1280, 128), bf), vm((8, 32, 640), bf), vm((8, 32, 640), bf),
            vm((CH, 8, 32, CW), bf), vm((CH, 8, 32, CW), bf), vm((CH, 512, CW), bf), vm((CH, 256, CW), bf), vm((CH, 256, CW), bf),
            dma((6, 2, 8)), dma((6, 2, 8)), dma((17, 6)), dma((17, 6)), dma((CH, 2, 8)), dma((CH, 2, 8)),
            dma((8,)), dma((8,)), dma((16,)), dma((2, 16)), dma((4,)), dma((4,)),
            dma((8,)), dma((8,)), dma((8,)), dma((8,)),
            dma((17,)), dma((17,)), dma((8,)), dma((8,)), dma((8,)), dma((8,)),
            dma((CH, 8)), dma((CH, 8)), dma((CH, 8)), dma((CH, 8)),
        ],
        compiler_params=pltpu.CompilerParams(collective_id=1, has_side_effects=True, vmem_limit_bytes=60 << 20),
    )(*operands)


def per_device(
    tokens, qkv_weight, out_weight, merge_weight, ln_gains, segments, merge_rows, owners
):
    fs = lax.axis_index("fsdp")
    z = lax.axis_index("yz") % NZ
    q_in = qkv_weight.reshape(3, 10, 2, 160).transpose(2, 1, 0, 3).reshape(2, 10, 480)
    q_in = jnp.pad(q_in, ((0, 0), (0, 6), (0, 32)))
    o_flat = out_weight.T
    o_in = jnp.where(fs % 2 == 0, jnp.pad(o_flat, ((0, 6), (0, 64))), jnp.pad(o_flat, ((0, 6), (64, 0))))
    m_in = jnp.pad(merge_weight, ((0, 6), (0, 0)))
    seg_in = jnp.broadcast_to(segments, (8, 128))
    order = merge_rows[0].reshape(32, 4).T.reshape(128, 1)
    order_in = jnp.broadcast_to(order, (128, 128))
    targets = owners[:, 0]
    ranks = jnp.arange(32)
    earlier = (targets[:, None] == targets[None, :]) & (ranks[None, :] < ranks[:, None])
    slot_row = targets * 2 + jnp.sum(earlier.astype(jnp.int32), axis=1) + 1
    spread = jnp.where(jnp.arange(4)[:, None] == z % 4, slot_row[None, :], 0).reshape(1, 128)
    slot_in = jnp.broadcast_to(spread, (8, 128))
    return block(tokens, ln_gains, q_in, o_in, m_in, seg_in, order_in, slot_in)


def solution(mesh):
    cut = Mesh(mesh.devices.reshape(2, 64, 4), ("xh", "yz", "fsdp"))
    every = ("xh", "yz", "fsdp")
    return jax.shard_map(
        per_device,
        mesh=cut,
        in_specs=(
            P(every, None),
            P(None, ("xh", "yz"), "fsdp"),
            P("fsdp", ("xh", "yz")),
            P(every, None),
            P(),
            P(("xh", "yz"), "fsdp"),
            P(every, None),
            P(every, None),
        ),
        out_specs=P(every, None),
        check_vma=False,
    )
```

```python
import math

import jax
import jax.numpy as jnp
from jax import lax
from jax.experimental import pallas as pl
from jax.experimental.pallas import tpu as pltpu
from jax.sharding import Mesh
from jax.sharding import PartitionSpec as P

HD = 80
NZ = 16
NY = 4
CH = 5
CW = 256
MESH = pl.DeviceIdType.MESH
epsilon = 1e-06


def coords():
    yz = lax.axis_index("yz")
    return lax.axis_index("xh"), yz // NZ, yz % NZ, lax.axis_index("fsdp")


def rows_of(place, n):
    return pl.ds(pl.multiple_of(place * n, n), n)


def center(values):
    middle = values - jnp.mean(values, axis=1, keepdims=True)
    variance = jnp.mean(middle * middle, axis=1, keepdims=True)
    return middle * lax.rsqrt(variance + epsilon)


def mix(left, right):
    return jnp.dot(left, right, preferred_element_type=jnp.float32)


def mix_t(left, right):
    return lax.dot_general(left, right, (((1,), (1,)), ((), ())), preferred_element_type=jnp.float32)


def block_kernel(
    tok_in, gain_in, q_in, o_in, m_in, seg_row, order_row, owner_col, out, seg_in,
    wq, wo, wm, unmove, tok_t, normed_all, seg_all, q_box, o_box, m_box, slots,
    qkv, att_out, att_in, mi_out, mi_in, part_out, part_in, rows, picked1, picked2, picked3, landed1, landed2, landed3,
    c_send, c_recv, y_send, y_recv, e_send, e_recv,
    q_send, q_recv, o_send, o_recv, m_send, m_recv, n_send, n_recv, g_send, g_recv,
    s_send, s_recv, a_send, a_recv, i_send, i_recv, r_send, r_recv, p_send, p_recv,
):
    bf = jnp.bfloat16
    xh, y, z, fs = coords()
    core = fs % 2
    xlo = fs // 2
    mine = xh * 4 + y
    member = xh * 4 + fs
    up, below = (z + 1) % NZ, (z + NZ - 1) % NZ

    def dev(xh_, y_, z_, fs_):
        return (xh_, y_ * NZ + z_, fs_)

    barrier = pltpu.get_barrier_semaphore()
    for dx in range(2):
        for dy in range(4):
            for df in range(4):
                if dx or dy or df:
                    there = dev((xh + dx) % 2, (y + dy) % 4, z, (fs + df) % 4)
                    pl.semaphore_signal(barrier, inc=1, device_id=there, device_id_type=MESH)
    for peer in (up, below):
        pl.semaphore_signal(barrier, inc=1, device_id=dev(xh, y, peer, fs), device_id_type=MESH)

    lane = lax.broadcasted_iota(jnp.int32, (128, 128), 1)
    for b in range(10):
        p = lax.broadcasted_iota(jnp.int32, (128, 128), 0) + b * 128
        pz = ((p >> 4) * 52429) >> 18
        rest = p - pz * 80
        tens = (rest * 52429) >> 19
        natural = (tens * NZ + pz) * 10 + (rest - tens * 10)
        for t in range(10):
            unmove[b * 128 : (b + 1) * 128, t * 128 : (t + 1) * 128] = jnp.where(
                natural == lane + t * 128, 1.0, 0.0
            ).astype(bf)
    normed = (center(tok_in[...].astype(jnp.float32)) * gain_in[0:1, :]).astype(bf)
    normed_all[member] = mix_t(normed, unmove[...]).astype(bf)
    seg_in[...] = jnp.broadcast_to(seg_row[...], (8, 128))
    seg_all[member] = seg_in[...]
    down_owner = jnp.broadcast_to(owner_col[...], (32, 128)).astype(jnp.float32)
    over_owner = jnp.concatenate([down_owner] * 4, axis=0).T
    over_owner = jnp.concatenate([over_owner[0:32, 0:32]] * 4, axis=1)
    lane32 = lax.broadcasted_iota(jnp.int32, (32, 128), 1) & 31
    earlier = (down_owner == over_owner) & (lax.broadcasted_iota(jnp.int32, (32, 128), 0) < lane32)
    rank = jnp.sum(jnp.where(earlier, 1.0, 0.0), axis=0, keepdims=True)
    slot_row = (over_owner[0:1, :] * 2.0 + rank + 1.0).astype(jnp.int32)
    slots[z] = jnp.broadcast_to(slot_row, (8, 128))
    pl.semaphore_wait(barrier, 33)

    def copy(src, dst, ssem, rsem, where):
        return pltpu.make_async_remote_copy(
            src_ref=src, dst_ref=dst, send_sem=ssem, recv_sem=rsem, device_id=where, device_id_type=MESH
        )

    def q_copy(step):
        dx, dy = step // 4, step % 4
        oxh, oy = (xh + dx) % 2, (y + dy) % 4
        return copy(q_in.at[oxh], q_box.at[mine], q_send.at[step], q_recv.at[step], dev(oxh, oy, z, fs))

    def q_arrival(step):
        dx, dy = step // 4, step % 4
        oxh, oy = (xh + dx) % 2, (y + 4 - dy) % 4
        return copy(q_in.at[xh], q_box.at[oxh * 4 + oy], q_send.at[step], q_recv.at[step], dev(oxh, oy, z, fs))

    for step in range(1, 8):
        q_copy(step).start()
    q_box[mine] = q_in[xh]

    o_steps = [(dx, dl, dy) for dx in range(2) for dl in range(2) for dy in range(4)]

    def o_slot(c, d):
        return o_box.at[c, d]

    def o_copy(k):
        dx, dl, dy = o_steps[k]
        oxh, olo, oy = (xh + dx) % 2, (xlo + dl) % 2, (y + dy) % 4
        return copy(o_in, o_slot(core, mine), o_send.at[k], o_recv.at[core, k], dev(oxh, oy, z, olo * 2 + xlo))

    def o_arrival(c, k):
        dx, dl, dy = o_steps[k]
        oxh, oy = (xh + dx) % 2, (y + 4 - dy) % 4
        return copy(o_in, o_slot(c, oxh * 4 + oy), o_send.at[k], o_recv.at[c, k], dev(oxh, oy, z, core * 2 + c))

    def o_remote(k):
        dx, dl, dy = o_steps[k]
        if dx or dy:
            return None
        return (xlo + dl) % 2 * 2 + xlo != fs

    for k in range(16):
        cond = o_remote(k)
        if cond is None:
            o_copy(k).start()
        else:
            @pl.when(cond)
            def _():
                o_copy(k).start()

    @pl.when(xlo == core)
    def _():
        o_box[core, mine] = o_in[...]

    def m_copy(dy):
        oy = (y + dy) % 4
        there = dev(xh, oy, z, y)
        return (
            copy(m_in.at[:, pl.ds(pl.multiple_of(oy * 256, 256), 256)], m_box.at[0, fs], m_send.at[0, dy], m_recv.at[0, fs], there),
            copy(m_in.at[:, pl.ds(1024, 256)], m_box.at[1, fs], m_send.at[1, dy], m_recv.at[1, fs], there),
        )

    def m_arrival(j):
        there = dev(xh, fs, z, j)
        return [
            copy(m_in.at[:, pl.ds(1024, 256)], m_box.at[half, j], m_send.at[half, 0], m_recv.at[half, j], there)
            for half in range(2)
        ]

    for dy in range(1, 4):
        for one in m_copy(dy):
            one.start()

    @pl.when(fs != y)
    def _():
        for one in m_copy(0):
            one.start()

    @pl.when(fs == y)
    def _():
        m_box[0, fs] = m_in[:, pl.ds(pl.multiple_of(y * 256, 256), 256)]
        m_box[1, fs] = m_in[:, 1024:1280]

    sibling = dev(xh, y, z, xlo * 2 + 1 - core)
    spot = xh * 2 + xlo

    def n_copy(dx, to):
        other = (spot + dx) % 4 if to else (spot + 4 - dx) % 4
        oxh, ofs = other // 2, other % 2 * 2 + core
        slot = member if to else oxh * 4 + ofs
        return copy(normed_all.at[member], normed_all.at[slot], n_send.at[dx], n_recv.at[dx], dev(oxh, y, z, ofs))

    def n_share(dx, to):
        other = (spot + 4 - dx) % 4
        slot = other // 2 * 4 + other % 2 * 2 + (core if to else 1 - core)
        return copy(normed_all.at[slot], normed_all.at[slot], n_send.at[4 + dx], n_recv.at[4 + dx], sibling)

    def g_copy(step, to):
        dx, df = step // 4, step % 4
        oxh = (xh + dx) % 2
        ofs = (fs + df) % 4 if to else (fs + 4 - df) % 4
        slot = member if to else oxh * 4 + ofs
        return copy(seg_in, seg_all.at[slot], g_send.at[step], g_recv.at[step], dev(oxh, y, z, ofs))

    for dx in (1, 3, 2):
        n_copy(dx, True).start()
    n_share(0, True).start()
    for step in range(1, 8):
        g_copy(step, True).start()

    def ten(count, depth):
        place = lax.broadcasted_iota(jnp.int32, (count, depth), 0)
        column = lax.broadcasted_iota(jnp.int32, (count, depth), 1)
        tens = (place * 52429) >> 19
        return jnp.where(column == tens * 16 + (place - tens * 10), 1.0, 0.0).astype(bf)

    def settle(picker, block):
        return mix(picker, block).astype(bf)

    pick80 = ten(80, 128)
    for step in range(1, 8):
        q_arrival(step).wait_recv()
    wq[z] = settle(pick80, q_box[...].reshape(128, 512))

    last = (8, 7)
    o_tile = y + y // 2
    o_part = pl.ds(pl.multiple_of(o_tile * 128, 128), 128)
    m_part = pl.ds(pl.multiple_of(y * 256, 256), 256)
    views = (
        lambda src: wq.at[src],
        lambda src: wo.at[core, src, :, o_part],
        lambda src: wo.at[core, src, :, pl.ds(256, 128)],
        lambda src: wm.at[src, :, m_part],
        lambda src: wm.at[src, :, pl.ds(1024, 256)],
        lambda src: slots.at[src],
    )

    def block_at(way, gone):
        return (z + NZ - gone) % NZ if way == 0 else (z + gone) % NZ

    def ring(k, way, step, arriving):
        view = views[k](block_at(way, step if arriving else step - 1))
        where = dev(xh, y, up if way == 0 else below, fs)
        return copy(view, view, c_send.at[k, way, step - 1], c_recv.at[k, way, step - 1], where)

    def begin(k):
        for way in range(2):
            ring(k, way, 1, False).start()

    def share(half, place, slot):
        return copy(wo.at[half, place], wo.at[half, place], s_send.at[slot], s_recv.at[slot], sibling)

    def o_along(place, slot, dy, to):
        oy = (y + dy) % 4 if to else (y + 4 - dy) % 4
        part = o_part if to else pl.ds(pl.multiple_of((oy + oy // 2) * 128, 128), 128)
        view = wo.at[core, place, :, part]
        return copy(view, view, y_send.at[slot, dy - 1], y_recv.at[slot, dy - 1], dev(xh, oy, z, fs))

    def m_along(place, slot, dy, to):
        oy = (y + dy) % 4 if to else (y + 4 - dy) % 4
        part = m_part if to else pl.ds(pl.multiple_of(oy * 256, 256), 256)
        view = wm.at[place, :, part]
        return copy(view, view, y_send.at[slot, dy + 2], y_recv.at[slot, dy + 2], dev(xh, oy, z, fs))

    def places(step):
        if step == 0:
            return [(z, 0)]
        return [(block_at(way, step), step + 8 * way) for way in range(2) if step <= last[way]]

    def serve(step):
        for k in (0, 1, 3, 2, 4, 5):
            for way in range(2):
                if step <= last[way]:
                    ring(k, way, step, True).wait_recv()
                    if step < last[way]:
                        ring(k, way, step + 1, False).start()

    def spread_out(step):
        for place, slot in places(step):
            for dy in (1, 3, 2):
                o_along(place, slot, dy, True).start()
        for place, slot in places(step):
            for dy in (1, 3, 2):
                m_along(place, slot, dy, True).start()

    def pass_on(step):
        for place, slot in places(step):
            for dy in range(1, 4):
                o_along(place, slot, dy, False).wait_recv()
            share(core, place, slot).start()

    begin(0)
    begin(5)
    for c in range(2):
        for k in range(16):
            dx, dl, dy = o_steps[k]
            here = (core + dl) % 2 == xlo
            cond = here if dx or dy else here & (core * 2 + c != fs)

            @pl.when(cond)
            def _():
                o_arrival(c, k).wait_recv()
    wo[core, z, :, 256:384] = settle(pick80, (o_box[0, :, :, 256:384] + o_box[1, :, :, 0:128]).reshape(128, 128))
    from_lane = pl.ds(pl.multiple_of((y % 2 + y // 2) * 128, 128), 128)
    wo[core, z, :, o_part] = settle(pick80, o_box[y // 2, :, :, from_lane].reshape(128, 128))
    begin(1)
    begin(2)
    for j in range(4):
        @pl.when((j != fs) | (y != fs))
        def _():
            for one in m_arrival(j):
                one.wait_recv()
    pick40 = ten(40, 64)
    wm[z, :, m_part] = settle(pick40, m_box[0].reshape(64, 256))
    wm[z, :, 1024:1280] = settle(pick40, m_box[1].reshape(64, 256))
    begin(3)
    begin(4)
    spread_out(0)
    tok_t[...] = mix_t(unmove[...], tok_in[...]).astype(bf)

    for step in range(1, 9):
        serve(step)
        spread_out(step)
        pass_on(step - 1)
        if step == 4:
            for dx in (1, 3):
                n_copy(dx, False).wait_recv()
                n_share(dx, True).start()
        if step == 6:
            n_copy(2, False).wait_recv()
            n_share(2, True).start()
    for dx in range(4):
        n_share(dx, False).wait_recv()
    for step in range(1, 8):
        g_copy(step, False).wait_recv()

    factor = 1.0 / math.sqrt(HD)

    def a_copy(step, to):
        dx, df = step // 4, step % 4
        oxh = (xh + dx) % 2
        ofs = (fs + df) % 4 if to else (fs + 4 - df) % 4
        head = fs * 2 + xh if to else ofs * 2 + oxh
        return copy(
            att_out.at[oxh * 4 + ofs], att_in.at[rows_of(head, 160), :], a_send.at[step], a_recv.at[step], dev(oxh, y, z, ofs)
        )

    def project(g):
        block = normed_all[pl.ds(g * 4, 4)].reshape(512, 1280)
        qkv[...] = mix(block, wq[...].reshape(1280, 512)).astype(bf)

    def attend(g):
        names = [seg_all[g * 4 + b][0:1, :].astype(jnp.float32) for b in range(4)]
        downs = [jnp.concatenate([jnp.broadcast_to(one, (128, 128)).T] * 4, axis=1) for one in names]
        allowed = jnp.concatenate(downs, axis=0) == jnp.concatenate(names, axis=1)
        for h in range(2):
            query = qkv[:, h * HD : h * HD + HD]
            key = qkv[:, 160 + h * HD : 160 + h * HD + HD]
            value = qkv[:, 320 + h * HD : 320 + h * HD + HD]
            scores = jnp.where(allowed, mix_t(key, query) * factor, -jnp.inf)
            weights = jnp.exp(scores - jnp.max(scores, axis=0, keepdims=True))
            totals = jnp.sum(weights, axis=0, keepdims=True)
            value_t = value.astype(jnp.float32).T.astype(bf)
            head_out = (mix(value_t, weights.astype(bf)) / totals).astype(bf)
            for b in range(4):
                att_out[g * 4 + b, h * HD : h * HD + HD, :] = head_out[:, b * 128 : (b + 1) * 128]

    project(1 - xh)
    attend(1 - xh)
    for step in range(4, 8):
        a_copy(step, True).start()
    project(xh)
    attend(xh)
    att_in[rows_of(fs * 2 + xh, 160), :] = att_out[member]
    for step in range(1, 4):
        a_copy(step, True).start()
    pass_on(8)
    for step in range(1, 8):
        a_copy(step, False).wait_recv()
    for step in range(9):
        for place, slot in places(step):
            share(1 - core, place, slot).wait_recv()

    update = mix(wo[0].reshape(1280, 640), att_in[0:640, :]) + mix(wo[1].reshape(1280, 640), att_in[640:1280, :])
    layer_t = (tok_t[...].astype(jnp.float32) + update).astype(bf)
    down = lax.broadcasted_iota(jnp.int32, (128, 128), 0)
    named = jnp.where(order_row[...] == down, 1.0, 0.0).astype(bf)
    regular = jnp.where(lane == ((down & 31) << 2) + (down >> 5), 1.0, 0.0).astype(bf)
    picker = mix_t(regular, named).astype(bf)
    chosen = mix_t(picker, layer_t).astype(bf)
    merge_in = (center(mix(chosen, unmove[...])) * gain_in[1:2, :]).astype(bf)
    for b in range(8):
        mi_out[b] = merge_in[b // 2 * 32 : b // 2 * 32 + 32, b % 2 * 640 : b % 2 * 640 + 640]

    def i_copy(step, to):
        dx, df = step // 4, step % 4
        oxh = (xh + dx) % 2
        ofs = (fs + df) % 4 if to else (fs + 4 - df) % 4
        other = oxh * 4 + ofs
        slot = member if to else other
        return copy(mi_out.at[other], mi_in.at[slot], i_send.at[step], i_recv.at[step], dev(oxh, y, z, ofs))

    for step in range(1, 8):
        i_copy(step, True).start()
    mi_in[member] = mi_out[member]
    for step in range(9):
        for place, slot in places(step):
            for dy in range(1, 4):
                m_along(place, slot, dy, False).wait_recv()
    for step in range(1, 8):
        i_copy(step, False).wait_recv()

    def r_copy(c, step, to):
        dx, df = step // 4, step % 4
        oxh = (xh + dx) % 2
        ofs = (fs + df) % 4 if to else (fs + 4 - df) % 4
        other = oxh * 4 + ofs
        slot = member if to else other
        return copy(
            part_out.at[c, other], part_in.at[c, slot], r_send.at[c, step], r_recv.at[c, step], dev(oxh, y, z, ofs)
        )

    inputs = mi_in[...].reshape(256, 640)
    for c in range(CH):
        part = mix(inputs, wm[:, :, c * CW : (c + 1) * CW].reshape(640, CW)).astype(bf)
        part_out[c] = part.reshape(8, 32, CW)
        for step in range(1, 8):
            r_copy(c, step, True).start()
        part_in[c, member] = part_out[c, member]

    def seat(way, gone):
        return 0 if gone == 0 else 15 if gone == 8 else 2 * gone - 1 + way

    def e_copy(c, way, step):
        where = dev(xh, y, up if way == 0 else below, fs)
        return copy(
            rows.at[c, seat(way, step - 1)], rows.at[c, seat(way, step)], e_send.at[c, way, step - 1], e_recv.at[c, way, step - 1], where
        )

    for c in range(CH):
        for step in range(1, 8):
            r_copy(c, step, False).wait_recv()
        rows[c, 0] = jnp.sum(part_in[c].astype(jnp.float32), axis=0).astype(bf)
        for way in range(2):
            e_copy(c, way, 1).start()

    parts = ((0, 8, 4), (8, 4, 6), (12, 4, 8))
    boxes = ((picked1, landed1), (picked2, landed2), (picked3, landed3))

    def p_copy(part, c, step, to):
        dx, dy = step // 4, step % 4
        oxh = (xh + dx) % 2
        oy = (y + dy) % 4 if to else (y + 4 - dy) % 4
        other = oxh * 4 + oy
        slot = mine if to else other
        gone, come = boxes[part]
        return copy(
            gone.at[c, other], come.at[c, slot], p_send.at[part, c, step], p_recv.at[part, c, step], dev(oxh, oy, z, fs)
        )

    row_keys = []
    lane_row = lax.broadcasted_iota(jnp.int32, (1, 128), 1)
    for q in range(4):
        row_key = jnp.zeros((1, 128), jnp.int32)
        for i in range(4):
            number = 4 * q + i
            gone = (number + 1) // 2
            source = block_at(0, gone) if number % 2 else block_at(1, gone)
            row_key = jnp.where((lane_row >> 5) == i, slots[source][0:1, :], row_key)
        row_keys.append(row_key)
    selects, turns = [], []
    for first, count, _ in parts:
        shape = (16 * count, 32 * count)
        bits = 4 if count == 8 else 3
        place = lax.broadcasted_iota(jnp.int32, shape, 0)
        column = lax.broadcasted_iota(jnp.int32, shape, 1)
        wanted = ((place >> bits) << 5) + 2 * z + (place & 1) + 1
        keys = jnp.concatenate(row_keys[first // 4 : (first + count) // 4], axis=1)
        match = (((place >> 1) & (count - 1)) == (column >> 5)) & (keys == wanted)
        selects.append(jnp.where(match, 1.0, 0.0).astype(bf))
        shape = (256, 16 * count)
        place = lax.broadcasted_iota(jnp.int32, shape, 0)
        column = lax.broadcasted_iota(jnp.int32, shape, 1)
        number = ((column >> 1) & (count - 1)) + first
        gone = (number + 1) >> 1
        source = (z + jnp.where((number & 1) == 1, NZ - gone, gone)) & 15
        match = ((place >> 5) == (column >> bits)) & ((place & 1) == (column & 1)) & (((place >> 1) & 15) == source)
        turns.append(jnp.where(match, 1.0, 0.0).astype(bf))
    for step in range(1, 9):
        for c in range(CH):
            for way in range(2):
                if step <= last[way]:
                    e_copy(c, way, step).wait_recv()
                    if step < last[way]:
                        e_copy(c, way, step + 1).start()
            if step == 8:
                first, count, _ = parts[2]
                block = mix(selects[2], rows[c, first : first + count].reshape(32 * count, CW)).astype(bf)
                boxes[2][0][c] = block.reshape(8, 2 * count, CW)
                for hop in range(1, 8):
                    p_copy(2, c, hop, True).start()
        for part in range(2):
            first, count, ready = parts[part]
            if step == ready:
                for c in range(CH):
                    block = mix(selects[part], rows[c, first : first + count].reshape(32 * count, CW)).astype(bf)
                    boxes[part][0][c] = block.reshape(8, 2 * count, CW)
                    for hop in range(1, 8):
                        p_copy(part, c, hop, True).start()
    for c in range(CH):
        total = None
        for part in range(3):
            gone, come = boxes[part]
            come[c, mine] = gone[c, mine]
            for step in range(1, 8):
                p_copy(part, c, step, False).wait_recv()
            block = mix(turns[part], come[c].reshape(16 * parts[part][1], CW))
            total = block if total is None else total + block
        out[:, c * CW : (c + 1) * CW] = total.astype(bf)

    for step in range(1, 8):
        q_copy(step).wait_send()
        g_copy(step, True).wait_send()
        a_copy(step, True).wait_send()
        i_copy(step, True).wait_send()
        for c in range(CH):
            r_copy(c, step, True).wait_send()
            for part in range(3):
                p_copy(part, c, step, True).wait_send()
    for dx in range(4):
        n_share(dx, True).wait_send()
        if dx:
            n_copy(dx, True).wait_send()
    for k in range(16):
        cond = o_remote(k)
        if cond is None:
            o_copy(k).wait_send()
        else:
            @pl.when(cond)
            def _():
                o_copy(k).wait_send()
    for dy in range(1, 4):
        for one in m_copy(dy):
            one.wait_send()

    @pl.when(fs != y)
    def _():
        for one in m_copy(0):
            one.wait_send()

    for way in range(2):
        for step in range(1, last[way] + 1):
            for k in range(6):
                ring(k, way, step, False).wait_send()
            for c in range(CH):
                e_copy(c, way, step).wait_send()
    for step in range(9):
        for place_, slot in places(step):
            share(core, place_, slot).wait_send()
            for dy in range(1, 4):
                o_along(place_, slot, dy, True).wait_send()
                m_along(place_, slot, dy, True).wait_send()


def block(*operands):
    bf = jnp.bfloat16
    dma = pltpu.SemaphoreType.DMA
    vm = pltpu.VMEM
    return pl.pallas_call(
        block_kernel,
        out_shape=jax.ShapeDtypeStruct((256, 1280), bf),
        in_specs=[pl.BlockSpec(memory_space=pltpu.VMEM)] * 8,
        out_specs=pl.BlockSpec(memory_space=pltpu.VMEM),
        scratch_shapes=[
            vm((8, 128), jnp.int32), vm((NZ, 80, 512), bf), vm((2, NZ, 80, 640), bf), vm((NZ, 40, 1280), bf), vm((1280, 1280), bf),
            vm((1280, 128), bf), vm((8, 128, 1280), bf), vm((8, 8, 128), jnp.int32),
            vm((8, 16, 512), bf), vm((2, 8, 16, 384), bf), vm((2, 4, 16, 256), bf), vm((NZ, 8, 128), jnp.int32),
            vm((512, 512), bf), vm((8, 160, 128), bf), vm((1280, 128), bf), vm((8, 32, 640), bf), vm((8, 32, 640), bf),
            vm((CH, 8, 32, CW), bf), vm((CH, 8, 32, CW), bf), vm((CH, NZ, 32, CW), bf),
            vm((CH, 8, 16, CW), bf), vm((CH, 8, 8, CW), bf), vm((CH, 8, 8, CW), bf), vm((CH, 8, 16, CW), bf), vm((CH, 8, 8, CW), bf), vm((CH, 8, 8, CW), bf),
            dma((6, 2, 8)), dma((6, 2, 8)), dma((17, 6)), dma((17, 6)), dma((CH, 2, 8)), dma((CH, 2, 8)),
            dma((8,)), dma((8,)), dma((16,)), dma((2, 16)), dma((2, 4)), dma((2, 4)),
            dma((8,)), dma((8,)), dma((8,)), dma((8,)),
            dma((17,)), dma((17,)), dma((8,)), dma((8,)), dma((8,)), dma((8,)),
            dma((CH, 8)), dma((CH, 8)), dma((3, CH, 8)), dma((3, CH, 8)),
        ],
        compiler_params=pltpu.CompilerParams(collective_id=1, has_side_effects=True, vmem_limit_bytes=60 << 20),
    )(*operands)


def per_device(
    tokens, qkv_weight, out_weight, merge_weight, ln_gains, segments, merge_rows, owners
):
    fs = lax.axis_index("fsdp")
    q_in = qkv_weight.reshape(3, 10, 2, 160).transpose(2, 1, 0, 3).reshape(2, 10, 480)
    q_in = jnp.pad(q_in, ((0, 0), (0, 6), (0, 32)))
    o_flat = out_weight.T
    o_in = jnp.where(fs % 2 == 0, jnp.pad(o_flat, ((0, 6), (0, 64))), jnp.pad(o_flat, ((0, 6), (64, 0))))
    m_in = jnp.pad(merge_weight, ((0, 6), (0, 0)))
    return block(tokens, ln_gains, q_in, o_in, m_in, segments, merge_rows, owners)


def solution(mesh):
    cut = Mesh(mesh.devices.reshape(2, 64, 4), ("xh", "yz", "fsdp"))
    every = ("xh", "yz", "fsdp")
    return jax.shard_map(
        per_device,
        mesh=cut,
        in_specs=(
            P(every, None),
            P(None, ("xh", "yz"), "fsdp"),
            P("fsdp", ("xh", "yz")),
            P(every, None),
            P(),
            P(("xh", "yz"), "fsdp"),
            P(every, None),
            P(every, None),
        ),
        out_specs=P(every, None),
        check_vma=False,
    )
```

```python
import math

import jax
import jax.numpy as jnp
from jax import lax
from jax.experimental import pallas as pl
from jax.experimental.pallas import tpu as pltpu
from jax.sharding import Mesh
from jax.sharding import PartitionSpec as P

HD = 80
NZ = 16
NY = 4
CH = 5
CW = 256
MESH = pl.DeviceIdType.MESH
epsilon = 1e-06


def coords():
    yz = lax.axis_index("yz")
    return lax.axis_index("xh"), yz // NZ, yz % NZ, lax.axis_index("fsdp")


def rows_of(place, n):
    return pl.ds(pl.multiple_of(place * n, n), n)


def center(values):
    middle = values - jnp.mean(values, axis=1, keepdims=True)
    variance = jnp.mean(middle * middle, axis=1, keepdims=True)
    return middle * lax.rsqrt(variance + epsilon)


def mix(left, right):
    return jnp.dot(left, right, preferred_element_type=jnp.float32)


def mix_t(left, right):
    return lax.dot_general(left, right, (((1,), (1,)), ((), ())), preferred_element_type=jnp.float32)


def block_kernel(
    tok_in, gain_in, q_in, o_in, m_in, seg_row, order_row, owner_col, out, seg_in,
    wq, wo, wm, unmove, tok_t, normed_all, seg_all, q_box, o_box, m_box, slots,
    qkv, att_out, att_in, mi_out, mi_in, part_out, part_in, rows, picked1, picked2, picked3, landed1, landed2, landed3,
    c_send, c_recv, y_send, y_recv, e_send, e_recv,
    q_send, q_recv, o_send, o_recv, m_send, m_recv, n_send, n_recv, g_send, g_recv,
    s_send, s_recv, a_send, a_recv, i_send, i_recv, r_send, r_recv, p_send, p_recv,
):
    bf = jnp.bfloat16
    xh, y, z, fs = coords()
    core = fs % 2
    xlo = fs // 2
    mine = xh * 4 + y
    member = xh * 4 + fs
    up, below = (z + 1) % NZ, (z + NZ - 1) % NZ

    def dev(xh_, y_, z_, fs_):
        return (xh_, y_ * NZ + z_, fs_)

    barrier = pltpu.get_barrier_semaphore()
    for dx in range(2):
        for dy in range(4):
            for df in range(4):
                if dx or dy or df:
                    there = dev((xh + dx) % 2, (y + dy) % 4, z, (fs + df) % 4)
                    pl.semaphore_signal(barrier, inc=1, device_id=there, device_id_type=MESH)
    for peer in (up, below):
        pl.semaphore_signal(barrier, inc=1, device_id=dev(xh, y, peer, fs), device_id_type=MESH)

    lane = lax.broadcasted_iota(jnp.int32, (128, 128), 1)
    for b in range(10):
        p = lax.broadcasted_iota(jnp.int32, (128, 128), 0) + b * 128
        pz = ((p >> 4) * 52429) >> 18
        rest = p - pz * 80
        tens = (rest * 52429) >> 19
        natural = (tens * NZ + pz) * 10 + (rest - tens * 10)
        for t in range(10):
            unmove[b * 128 : (b + 1) * 128, t * 128 : (t + 1) * 128] = jnp.where(
                natural == lane + t * 128, 1.0, 0.0
            ).astype(bf)
    normed = (center(tok_in[...].astype(jnp.float32)) * gain_in[0:1, :]).astype(bf)
    normed_all[member] = mix_t(normed, unmove[...]).astype(bf)
    seg_in[...] = jnp.broadcast_to(seg_row[...], (8, 128))
    seg_all[member] = seg_in[...]
    down_owner = jnp.broadcast_to(owner_col[...], (32, 128)).astype(jnp.float32)
    over_owner = jnp.concatenate([down_owner] * 4, axis=0).T
    over_owner = jnp.concatenate([over_owner[0:32, 0:32]] * 4, axis=1)
    lane32 = lax.broadcasted_iota(jnp.int32, (32, 128), 1) & 31
    earlier = (down_owner == over_owner) & (lax.broadcasted_iota(jnp.int32, (32, 128), 0) < lane32)
    rank = jnp.sum(jnp.where(earlier, 1.0, 0.0), axis=0, keepdims=True)
    slot_row = (over_owner[0:1, :] * 2.0 + rank + 1.0).astype(jnp.int32)
    slots[z] = jnp.broadcast_to(slot_row, (8, 128))
    pl.semaphore_wait(barrier, 33)

    def copy(src, dst, ssem, rsem, where):
        return pltpu.make_async_remote_copy(
            src_ref=src, dst_ref=dst, send_sem=ssem, recv_sem=rsem, device_id=where, device_id_type=MESH
        )

    def q_copy(step):
        dx, dy = step // 4, step % 4
        oxh, oy = (xh + dx) % 2, (y + dy) % 4
        return copy(q_in.at[oxh], q_box.at[mine], q_send.at[step], q_recv.at[step], dev(oxh, oy, z, fs))

    def q_arrival(step):
        dx, dy = step // 4, step % 4
        oxh, oy = (xh + dx) % 2, (y + 4 - dy) % 4
        return copy(q_in.at[xh], q_box.at[oxh * 4 + oy], q_send.at[step], q_recv.at[step], dev(oxh, oy, z, fs))

    for step in range(1, 8):
        q_copy(step).start()
    q_box[mine] = q_in[xh]

    o_steps = [(dx, dl, dy) for dx in range(2) for dl in range(2) for dy in range(4)]

    def o_slot(c, d):
        return o_box.at[c, d]

    def o_copy(k):
        dx, dl, dy = o_steps[k]
        oxh, olo, oy = (xh + dx) % 2, (xlo + dl) % 2, (y + dy) % 4
        return copy(o_in, o_slot(core, mine), o_send.at[k], o_recv.at[core, k], dev(oxh, oy, z, olo * 2 + xlo))

    def o_arrival(c, k):
        dx, dl, dy = o_steps[k]
        oxh, oy = (xh + dx) % 2, (y + 4 - dy) % 4
        return copy(o_in, o_slot(c, oxh * 4 + oy), o_send.at[k], o_recv.at[c, k], dev(oxh, oy, z, core * 2 + c))

    def o_remote(k):
        dx, dl, dy = o_steps[k]
        if dx or dy:
            return None
        return (xlo + dl) % 2 * 2 + xlo != fs

    for k in range(16):
        cond = o_remote(k)
        if cond is None:
            o_copy(k).start()
        else:
            @pl.when(cond)
            def _():
                o_copy(k).start()

    @pl.when(xlo == core)
    def _():
        o_box[core, mine] = o_in[...]

    def m_copy(dy):
        oy = (y + dy) % 4
        there = dev(xh, oy, z, y)
        return (
            copy(m_in.at[:, pl.ds(pl.multiple_of(oy * 256, 256), 256)], m_box.at[0, fs], m_send.at[0, dy], m_recv.at[0, fs], there),
            copy(m_in.at[:, pl.ds(1024, 256)], m_box.at[1, fs], m_send.at[1, dy], m_recv.at[1, fs], there),
        )

    def m_arrival(j):
        there = dev(xh, fs, z, j)
        return [
            copy(m_in.at[:, pl.ds(1024, 256)], m_box.at[half, j], m_send.at[half, 0], m_recv.at[half, j], there)
            for half in range(2)
        ]

    for dy in range(1, 4):
        for one in m_copy(dy):
            one.start()

    @pl.when(fs != y)
    def _():
        for one in m_copy(0):
            one.start()

    @pl.when(fs == y)
    def _():
        m_box[0, fs] = m_in[:, pl.ds(pl.multiple_of(y * 256, 256), 256)]
        m_box[1, fs] = m_in[:, 1024:1280]

    sibling = dev(xh, y, z, xlo * 2 + 1 - core)
    spot = xh * 2 + xlo

    def n_copy(dx, to):
        other = (spot + dx) % 4 if to else (spot + 4 - dx) % 4
        oxh, ofs = other // 2, other % 2 * 2 + core
        slot = member if to else oxh * 4 + ofs
        return copy(normed_all.at[member], normed_all.at[slot], n_send.at[dx], n_recv.at[dx], dev(oxh, y, z, ofs))

    def n_share(dx, to):
        other = (spot + 4 - dx) % 4
        slot = other // 2 * 4 + other % 2 * 2 + (core if to else 1 - core)
        return copy(normed_all.at[slot], normed_all.at[slot], n_send.at[4 + dx], n_recv.at[4 + dx], sibling)

    def g_copy(step, to):
        dx, df = step // 4, step % 4
        oxh = (xh + dx) % 2
        ofs = (fs + df) % 4 if to else (fs + 4 - df) % 4
        slot = member if to else oxh * 4 + ofs
        return copy(seg_in, seg_all.at[slot], g_send.at[step], g_recv.at[step], dev(oxh, y, z, ofs))

    for dx in (1, 3, 2):
        n_copy(dx, True).start()
    n_share(0, True).start()
    for step in range(1, 8):
        g_copy(step, True).start()

    def ten(count, depth):
        place = lax.broadcasted_iota(jnp.int32, (count, depth), 0)
        column = lax.broadcasted_iota(jnp.int32, (count, depth), 1)
        tens = (place * 52429) >> 19
        return jnp.where(column == tens * 16 + (place - tens * 10), 1.0, 0.0).astype(bf)

    def settle(picker, block):
        return mix(picker, block).astype(bf)

    pick80 = ten(80, 128)
    for step in range(1, 8):
        q_arrival(step).wait_recv()
    wq[z] = settle(pick80, q_box[...].reshape(128, 512))

    last = (8, 7)
    o_tile = y + y // 2
    o_part = pl.ds(pl.multiple_of(o_tile * 128, 128), 128)
    m_part = pl.ds(pl.multiple_of(y * 256, 256), 256)
    views = (
        lambda src: wq.at[src],
        lambda src: wo.at[core, src, :, o_part],
        lambda src: wo.at[core, src, :, pl.ds(256, 128)],
        lambda src: wm.at[src, :, m_part],
        lambda src: wm.at[src, :, pl.ds(1024, 256)],
        lambda src: slots.at[src],
    )

    def block_at(way, gone):
        return (z + NZ - gone) % NZ if way == 0 else (z + gone) % NZ

    def ring(k, way, step, arriving):
        view = views[k](block_at(way, step if arriving else step - 1))
        where = dev(xh, y, up if way == 0 else below, fs)
        return copy(view, view, c_send.at[k, way, step - 1], c_recv.at[k, way, step - 1], where)

    def begin(k):
        for way in range(2):
            ring(k, way, 1, False).start()

    def share(half, place, slot):
        return copy(wo.at[half, place], wo.at[half, place], s_send.at[slot], s_recv.at[slot], sibling)

    def o_along(place, slot, dy, to):
        oy = (y + dy) % 4 if to else (y + 4 - dy) % 4
        part = o_part if to else pl.ds(pl.multiple_of((oy + oy // 2) * 128, 128), 128)
        view = wo.at[core, place, :, part]
        return copy(view, view, y_send.at[slot, dy - 1], y_recv.at[slot, dy - 1], dev(xh, oy, z, fs))

    def m_along(place, slot, dy, to):
        oy = (y + dy) % 4 if to else (y + 4 - dy) % 4
        part = m_part if to else pl.ds(pl.multiple_of(oy * 256, 256), 256)
        view = wm.at[place, :, part]
        return copy(view, view, y_send.at[slot, dy + 2], y_recv.at[slot, dy + 2], dev(xh, oy, z, fs))

    def places(step):
        if step == 0:
            return [(z, 0)]
        return [(block_at(way, step), step + 8 * way) for way in range(2) if step <= last[way]]

    def serve(step):
        for k in (0, 1, 3, 2, 4, 5):
            for way in range(2):
                if step <= last[way]:
                    ring(k, way, step, True).wait_recv()
                    if step < last[way]:
                        ring(k, way, step + 1, False).start()

    def spread_out(step):
        for place, slot in places(step):
            for dy in (1, 3, 2):
                o_along(place, slot, dy, True).start()
        for place, slot in places(step):
            for dy in (1, 3, 2):
                m_along(place, slot, dy, True).start()

    def pass_on(step):
        for place, slot in places(step):
            for dy in range(1, 4):
                o_along(place, slot, dy, False).wait_recv()
            share(core, place, slot).start()

    begin(0)
    begin(5)
    for c in range(2):
        for k in range(16):
            dx, dl, dy = o_steps[k]
            here = (core + dl) % 2 == xlo
            cond = here if dx or dy else here & (core * 2 + c != fs)

            @pl.when(cond)
            def _():
                o_arrival(c, k).wait_recv()
    wo[core, z, :, 256:384] = settle(pick80, (o_box[0, :, :, 256:384] + o_box[1, :, :, 0:128]).reshape(128, 128))
    from_lane = pl.ds(pl.multiple_of((y % 2 + y // 2) * 128, 128), 128)
    wo[core, z, :, o_part] = settle(pick80, o_box[y // 2, :, :, from_lane].reshape(128, 128))
    begin(1)
    begin(2)
    for j in range(4):
        @pl.when((j != fs) | (y != fs))
        def _():
            for one in m_arrival(j):
                one.wait_recv()
    pick40 = ten(40, 64)
    wm[z, :, m_part] = settle(pick40, m_box[0].reshape(64, 256))
    wm[z, :, 1024:1280] = settle(pick40, m_box[1].reshape(64, 256))
    begin(3)
    begin(4)
    spread_out(0)
    tok_t[...] = mix_t(unmove[...], tok_in[...]).astype(bf)

    for step in range(1, 9):
        serve(step)
        spread_out(step)
        if step > 1:
            pass_on(step - 2)
        if step == 4:
            for dx in (1, 3):
                n_copy(dx, False).wait_recv()
                n_share(dx, True).start()
        if step == 6:
            n_copy(2, False).wait_recv()
            n_share(2, True).start()
    for dx in range(4):
        n_share(dx, False).wait_recv()
    for step in range(1, 8):
        g_copy(step, False).wait_recv()

    factor = 1.0 / math.sqrt(HD)

    def a_copy(step, to):
        dx, df = step // 4, step % 4
        oxh = (xh + dx) % 2
        ofs = (fs + df) % 4 if to else (fs + 4 - df) % 4
        head = fs * 2 + xh if to else ofs * 2 + oxh
        return copy(
            att_out.at[oxh * 4 + ofs], att_in.at[rows_of(head, 160), :], a_send.at[step], a_recv.at[step], dev(oxh, y, z, ofs)
        )

    def project(g):
        block = normed_all[pl.ds(g * 4, 4)].reshape(512, 1280)
        qkv[...] = mix(block, wq[...].reshape(1280, 512)).astype(bf)

    def attend(g):
        names = [seg_all[g * 4 + b][0:1, :].astype(jnp.float32) for b in range(4)]
        downs = [jnp.concatenate([jnp.broadcast_to(one, (128, 128)).T] * 4, axis=1) for one in names]
        allowed = jnp.concatenate(downs, axis=0) == jnp.concatenate(names, axis=1)
        for h in range(2):
            query = qkv[:, h * HD : h * HD + HD]
            key = qkv[:, 160 + h * HD : 160 + h * HD + HD]
            value = qkv[:, 320 + h * HD : 320 + h * HD + HD]
            scores = jnp.where(allowed, mix_t(key, query) * factor, -jnp.inf)
            weights = jnp.exp(scores - jnp.max(scores, axis=0, keepdims=True))
            totals = jnp.sum(weights, axis=0, keepdims=True)
            value_t = value.astype(jnp.float32).T.astype(bf)
            head_out = (mix(value_t, weights.astype(bf)) / totals).astype(bf)
            for b in range(4):
                att_out[g * 4 + b, h * HD : h * HD + HD, :] = head_out[:, b * 128 : (b + 1) * 128]

    project(1 - xh)
    attend(1 - xh)
    for step in range(4, 8):
        a_copy(step, True).start()
    project(xh)
    attend(xh)
    att_in[rows_of(fs * 2 + xh, 160), :] = att_out[member]
    for step in range(1, 4):
        a_copy(step, True).start()
    pass_on(7)
    pass_on(8)
    for step in range(1, 8):
        a_copy(step, False).wait_recv()
    for step in range(9):
        for place, slot in places(step):
            share(1 - core, place, slot).wait_recv()

    update = mix(wo[0].reshape(1280, 640), att_in[0:640, :]) + mix(wo[1].reshape(1280, 640), att_in[640:1280, :])
    layer_t = (tok_t[...].astype(jnp.float32) + update).astype(bf)
    down = lax.broadcasted_iota(jnp.int32, (128, 128), 0)
    named = jnp.where(order_row[...] == down, 1.0, 0.0).astype(bf)
    regular = jnp.where(lane == ((down & 31) << 2) + (down >> 5), 1.0, 0.0).astype(bf)
    picker = mix_t(regular, named).astype(bf)
    chosen = mix_t(picker, layer_t).astype(bf)
    merge_in = (center(mix(chosen, unmove[...])) * gain_in[1:2, :]).astype(bf)
    for b in range(8):
        mi_out[b] = merge_in[b // 2 * 32 : b // 2 * 32 + 32, b % 2 * 640 : b % 2 * 640 + 640]

    def i_copy(step, to):
        dx, df = step // 4, step % 4
        oxh = (xh + dx) % 2
        ofs = (fs + df) % 4 if to else (fs + 4 - df) % 4
        other = oxh * 4 + ofs
        slot = member if to else other
        return copy(mi_out.at[other], mi_in.at[slot], i_send.at[step], i_recv.at[step], dev(oxh, y, z, ofs))

    for step in range(1, 8):
        i_copy(step, True).start()
    mi_in[member] = mi_out[member]
    for step in range(9):
        for place, slot in places(step):
            for dy in range(1, 4):
                m_along(place, slot, dy, False).wait_recv()
    for step in range(1, 8):
        i_copy(step, False).wait_recv()

    def r_copy(c, step, to):
        dx, df = step // 4, step % 4
        oxh = (xh + dx) % 2
        ofs = (fs + df) % 4 if to else (fs + 4 - df) % 4
        other = oxh * 4 + ofs
        slot = member if to else other
        return copy(
            part_out.at[c, other], part_in.at[c, slot], r_send.at[c, step], r_recv.at[c, step], dev(oxh, y, z, ofs)
        )

    inputs = mi_in[...].reshape(256, 640)
    for c in range(CH):
        part = mix(inputs, wm[:, :, c * CW : (c + 1) * CW].reshape(640, CW)).astype(bf)
        part_out[c] = part.reshape(8, 32, CW)
        for step in range(1, 8):
            r_copy(c, step, True).start()
        part_in[c, member] = part_out[c, member]

    def seat(way, gone):
        return 0 if gone == 0 else 15 if gone == 8 else 2 * gone - 1 + way

    def e_copy(c, way, step):
        where = dev(xh, y, up if way == 0 else below, fs)
        return copy(
            rows.at[c, seat(way, step - 1)], rows.at[c, seat(way, step)], e_send.at[c, way, step - 1], e_recv.at[c, way, step - 1], where
        )

    for c in range(CH):
        for step in range(1, 8):
            r_copy(c, step, False).wait_recv()
        rows[c, 0] = jnp.sum(part_in[c].astype(jnp.float32), axis=0).astype(bf)
        for way in range(2):
            e_copy(c, way, 1).start()

    parts = ((0, 8, 4), (8, 4, 6), (12, 4, 8))
    boxes = ((picked1, landed1), (picked2, landed2), (picked3, landed3))

    def p_copy(part, c, step, to):
        dx, dy = step // 4, step % 4
        oxh = (xh + dx) % 2
        oy = (y + dy) % 4 if to else (y + 4 - dy) % 4
        other = oxh * 4 + oy
        slot = mine if to else other
        gone, come = boxes[part]
        return copy(
            gone.at[c, other], come.at[c, slot], p_send.at[part, c, step], p_recv.at[part, c, step], dev(oxh, oy, z, fs)
        )

    row_keys = []
    lane_row = lax.broadcasted_iota(jnp.int32, (1, 128), 1)
    for q in range(4):
        row_key = jnp.zeros((1, 128), jnp.int32)
        for i in range(4):
            number = 4 * q + i
            gone = (number + 1) // 2
            source = block_at(0, gone) if number % 2 else block_at(1, gone)
            row_key = jnp.where((lane_row >> 5) == i, slots[source][0:1, :], row_key)
        row_keys.append(row_key)
    selects, turns = [], []
    for first, count, _ in parts:
        shape = (16 * count, 32 * count)
        bits = 4 if count == 8 else 3
        place = lax.broadcasted_iota(jnp.int32, shape, 0)
        column = lax.broadcasted_iota(jnp.int32, shape, 1)
        wanted = ((place >> bits) << 5) + 2 * z + (place & 1) + 1
        keys = jnp.concatenate(row_keys[first // 4 : (first + count) // 4], axis=1)
        match = (((place >> 1) & (count - 1)) == (column >> 5)) & (keys == wanted)
        selects.append(jnp.where(match, 1.0, 0.0).astype(bf))
        shape = (256, 16 * count)
        place = lax.broadcasted_iota(jnp.int32, shape, 0)
        column = lax.broadcasted_iota(jnp.int32, shape, 1)
        number = ((column >> 1) & (count - 1)) + first
        gone = (number + 1) >> 1
        source = (z + jnp.where((number & 1) == 1, NZ - gone, gone)) & 15
        match = ((place >> 5) == (column >> bits)) & ((place & 1) == (column & 1)) & (((place >> 1) & 15) == source)
        turns.append(jnp.where(match, 1.0, 0.0).astype(bf))
    for step in range(1, 9):
        for c in range(CH):
            for way in range(2):
                if step <= last[way]:
                    e_copy(c, way, step).wait_recv()
                    if step < last[way]:
                        e_copy(c, way, step + 1).start()
            if step == 8:
                first, count, _ = parts[2]
                block = mix(selects[2], rows[c, first : first + count].reshape(32 * count, CW)).astype(bf)
                boxes[2][0][c] = block.reshape(8, 2 * count, CW)
                for hop in range(1, 8):
                    p_copy(2, c, hop, True).start()
        for part in range(2):
            first, count, ready = parts[part]
            if step == ready:
                for c in range(CH):
                    block = mix(selects[part], rows[c, first : first + count].reshape(32 * count, CW)).astype(bf)
                    boxes[part][0][c] = block.reshape(8, 2 * count, CW)
                    for hop in range(1, 8):
                        p_copy(part, c, hop, True).start()
    for c in range(CH):
        total = None
        for part in range(3):
            gone, come = boxes[part]
            come[c, mine] = gone[c, mine]
            for step in range(1, 8):
                p_copy(part, c, step, False).wait_recv()
            block = mix(turns[part], come[c].reshape(16 * parts[part][1], CW))
            total = block if total is None else total + block
        out[:, c * CW : (c + 1) * CW] = total.astype(bf)

    for step in range(1, 8):
        q_copy(step).wait_send()
        g_copy(step, True).wait_send()
        a_copy(step, True).wait_send()
        i_copy(step, True).wait_send()
        for c in range(CH):
            r_copy(c, step, True).wait_send()
            for part in range(3):
                p_copy(part, c, step, True).wait_send()
    for dx in range(4):
        n_share(dx, True).wait_send()
        if dx:
            n_copy(dx, True).wait_send()
    for k in range(16):
        cond = o_remote(k)
        if cond is None:
            o_copy(k).wait_send()
        else:
            @pl.when(cond)
            def _():
                o_copy(k).wait_send()
    for dy in range(1, 4):
        for one in m_copy(dy):
            one.wait_send()

    @pl.when(fs != y)
    def _():
        for one in m_copy(0):
            one.wait_send()

    for way in range(2):
        for step in range(1, last[way] + 1):
            for k in range(6):
                ring(k, way, step, False).wait_send()
            for c in range(CH):
                e_copy(c, way, step).wait_send()
    for step in range(9):
        for place_, slot in places(step):
            share(core, place_, slot).wait_send()
            for dy in range(1, 4):
                o_along(place_, slot, dy, True).wait_send()
                m_along(place_, slot, dy, True).wait_send()


def block(*operands):
    bf = jnp.bfloat16
    dma = pltpu.SemaphoreType.DMA
    vm = pltpu.VMEM
    return pl.pallas_call(
        block_kernel,
        out_shape=jax.ShapeDtypeStruct((256, 1280), bf),
        in_specs=[pl.BlockSpec(memory_space=pltpu.VMEM)] * 8,
        out_specs=pl.BlockSpec(memory_space=pltpu.VMEM),
        scratch_shapes=[
            vm((8, 128), jnp.int32), vm((NZ, 80, 512), bf), vm((2, NZ, 80, 640), bf), vm((NZ, 40, 1280), bf), vm((1280, 1280), bf),
            vm((1280, 128), bf), vm((8, 128, 1280), bf), vm((8, 8, 128), jnp.int32),
            vm((8, 16, 512), bf), vm((2, 8, 16, 384), bf), vm((2, 4, 16, 256), bf), vm((NZ, 8, 128), jnp.int32),
            vm((512, 512), bf), vm((8, 160, 128), bf), vm((1280, 128), bf), vm((8, 32, 640), bf), vm((8, 32, 640), bf),
            vm((CH, 8, 32, CW), bf), vm((CH, 8, 32, CW), bf), vm((CH, NZ, 32, CW), bf),
            vm((CH, 8, 16, CW), bf), vm((CH, 8, 8, CW), bf), vm((CH, 8, 8, CW), bf), vm((CH, 8, 16, CW), bf), vm((CH, 8, 8, CW), bf), vm((CH, 8, 8, CW), bf),
            dma((6, 2, 8)), dma((6, 2, 8)), dma((17, 6)), dma((17, 6)), dma((CH, 2, 8)), dma((CH, 2, 8)),
            dma((8,)), dma((8,)), dma((16,)), dma((2, 16)), dma((2, 4)), dma((2, 4)),
            dma((8,)), dma((8,)), dma((8,)), dma((8,)),
            dma((17,)), dma((17,)), dma((8,)), dma((8,)), dma((8,)), dma((8,)),
            dma((CH, 8)), dma((CH, 8)), dma((3, CH, 8)), dma((3, CH, 8)),
        ],
        compiler_params=pltpu.CompilerParams(collective_id=1, has_side_effects=True, vmem_limit_bytes=60 << 20),
    )(*operands)


def per_device(
    tokens, qkv_weight, out_weight, merge_weight, ln_gains, segments, merge_rows, owners
):
    fs = lax.axis_index("fsdp")
    q_in = qkv_weight.reshape(3, 10, 2, 160).transpose(2, 1, 0, 3).reshape(2, 10, 480)
    q_in = jnp.pad(q_in, ((0, 0), (0, 6), (0, 32)))
    o_flat = out_weight.T
    o_in = jnp.where(fs % 2 == 0, jnp.pad(o_flat, ((0, 6), (0, 64))), jnp.pad(o_flat, ((0, 6), (64, 0))))
    m_in = jnp.pad(merge_weight, ((0, 6), (0, 0)))
    return block(tokens, ln_gains, q_in, o_in, m_in, segments, merge_rows, owners)


def solution(mesh):
    cut = Mesh(mesh.devices.reshape(2, 64, 4), ("xh", "yz", "fsdp"))
    every = ("xh", "yz", "fsdp")
    return jax.shard_map(
        per_device,
        mesh=cut,
        in_specs=(
            P(every, None),
            P(None, ("xh", "yz"), "fsdp"),
            P("fsdp", ("xh", "yz")),
            P(every, None),
            P(),
            P(("xh", "yz"), "fsdp"),
            P(every, None),
            P(every, None),
        ),
        out_specs=P(every, None),
        check_vma=False,
    )
```

```python
import math

import jax
import jax.numpy as jnp
from jax import lax
from jax.experimental import pallas as pl
from jax.experimental.pallas import tpu as pltpu
from jax.sharding import Mesh
from jax.sharding import PartitionSpec as P

HD = 80
NZ = 16
NY = 4
CH = 5
CW = 256
MESH = pl.DeviceIdType.MESH
epsilon = 1e-06


def coords():
    yz = lax.axis_index("yz")
    return lax.axis_index("xh"), yz // NZ, yz % NZ, lax.axis_index("fsdp")


def rows_of(place, n):
    return pl.ds(pl.multiple_of(place * n, n), n)


def center(values):
    middle = values - jnp.mean(values, axis=1, keepdims=True)
    variance = jnp.mean(middle * middle, axis=1, keepdims=True)
    return middle * lax.rsqrt(variance + epsilon)


def mix(left, right):
    return jnp.dot(left, right, preferred_element_type=jnp.float32)


def mix_t(left, right):
    return lax.dot_general(left, right, (((1,), (1,)), ((), ())), preferred_element_type=jnp.float32)


def block_kernel(
    tok_in, gain_in, q_in, o_in, m_in, seg_row, order_row, owner_col, out, seg_in,
    wq, wo, wm, unmove, tok_t, normed_all, seg_all, q_box, o_box, m_box, slots,
    qkv, att_out, att_in, mi_out, mi_in, part_out, part_in, rows, picked1, picked2, picked3, landed1, landed2, landed3,
    part_f, pair_out, pair_in, t_send, t_recv,
    c_send, c_recv, y_send, y_recv, e_send, e_recv,
    q_send, q_recv, o_send, o_recv, m_send, m_recv, n_send, n_recv, g_send, g_recv,
    s_send, s_recv, a_send, a_recv, i_send, i_recv, r_send, r_recv, p_send, p_recv,
):
    bf = jnp.bfloat16
    xh, y, z, fs = coords()
    core = fs % 2
    xlo = fs // 2
    mine = xh * 4 + y
    member = xh * 4 + fs
    up, below = (z + 1) % NZ, (z + NZ - 1) % NZ

    def dev(xh_, y_, z_, fs_):
        return (xh_, y_ * NZ + z_, fs_)

    barrier = pltpu.get_barrier_semaphore()
    for dx in range(2):
        for dy in range(4):
            for df in range(4):
                if dx or dy or df:
                    there = dev((xh + dx) % 2, (y + dy) % 4, z, (fs + df) % 4)
                    pl.semaphore_signal(barrier, inc=1, device_id=there, device_id_type=MESH)
    for peer in (up, below):
        pl.semaphore_signal(barrier, inc=1, device_id=dev(xh, y, peer, fs), device_id_type=MESH)

    lane = lax.broadcasted_iota(jnp.int32, (128, 128), 1)
    for b in range(10):
        p = lax.broadcasted_iota(jnp.int32, (128, 128), 0) + b * 128
        pz = ((p >> 4) * 52429) >> 18
        rest = p - pz * 80
        tens = (rest * 52429) >> 19
        natural = (tens * NZ + pz) * 10 + (rest - tens * 10)
        for t in range(10):
            unmove[b * 128 : (b + 1) * 128, t * 128 : (t + 1) * 128] = jnp.where(
                natural == lane + t * 128, 1.0, 0.0
            ).astype(bf)
    normed = (center(tok_in[...].astype(jnp.float32)) * gain_in[0:1, :]).astype(bf)
    normed_all[member] = mix_t(normed, unmove[...]).astype(bf)
    seg_in[...] = jnp.broadcast_to(seg_row[...], (8, 128))
    seg_all[member] = seg_in[...]
    down_owner = jnp.broadcast_to(owner_col[...], (32, 128)).astype(jnp.float32)
    over_owner = jnp.concatenate([down_owner] * 4, axis=0).T
    over_owner = jnp.concatenate([over_owner[0:32, 0:32]] * 4, axis=1)
    lane32 = lax.broadcasted_iota(jnp.int32, (32, 128), 1) & 31
    earlier = (down_owner == over_owner) & (lax.broadcasted_iota(jnp.int32, (32, 128), 0) < lane32)
    rank = jnp.sum(jnp.where(earlier, 1.0, 0.0), axis=0, keepdims=True)
    slot_row = (over_owner[0:1, :] * 2.0 + rank + 1.0).astype(jnp.int32)
    slots[z] = jnp.broadcast_to(slot_row, (8, 128))
    pl.semaphore_wait(barrier, 33)

    def copy(src, dst, ssem, rsem, where):
        return pltpu.make_async_remote_copy(
            src_ref=src, dst_ref=dst, send_sem=ssem, recv_sem=rsem, device_id=where, device_id_type=MESH
        )

    def q_copy(step):
        dx, dy = step // 4, step % 4
        oxh, oy = (xh + dx) % 2, (y + dy) % 4
        return copy(q_in.at[oxh], q_box.at[mine], q_send.at[step], q_recv.at[step], dev(oxh, oy, z, fs))

    def q_arrival(step):
        dx, dy = step // 4, step % 4
        oxh, oy = (xh + dx) % 2, (y + 4 - dy) % 4
        return copy(q_in.at[xh], q_box.at[oxh * 4 + oy], q_send.at[step], q_recv.at[step], dev(oxh, oy, z, fs))

    for step in range(1, 8):
        q_copy(step).start()
    q_box[mine] = q_in[xh]

    o_steps = [(dx, dl, dy) for dx in range(2) for dl in range(2) for dy in range(4)]

    def o_slot(c, d):
        return o_box.at[c, d]

    def o_copy(k):
        dx, dl, dy = o_steps[k]
        oxh, olo, oy = (xh + dx) % 2, (xlo + dl) % 2, (y + dy) % 4
        return copy(o_in, o_slot(core, mine), o_send.at[k], o_recv.at[core, k], dev(oxh, oy, z, olo * 2 + xlo))

    def o_arrival(c, k):
        dx, dl, dy = o_steps[k]
        oxh, oy = (xh + dx) % 2, (y + 4 - dy) % 4
        return copy(o_in, o_slot(c, oxh * 4 + oy), o_send.at[k], o_recv.at[c, k], dev(oxh, oy, z, core * 2 + c))

    def o_remote(k):
        dx, dl, dy = o_steps[k]
        if dx or dy:
            return None
        return (xlo + dl) % 2 * 2 + xlo != fs

    for k in range(16):
        cond = o_remote(k)
        if cond is None:
            o_copy(k).start()
        else:
            @pl.when(cond)
            def _():
                o_copy(k).start()

    @pl.when(xlo == core)
    def _():
        o_box[core, mine] = o_in[...]

    def m_copy(dy):
        oy = (y + dy) % 4
        there = dev(xh, oy, z, y)
        return (
            copy(m_in.at[:, pl.ds(pl.multiple_of(oy * 256, 256), 256)], m_box.at[0, fs], m_send.at[0, dy], m_recv.at[0, fs], there),
            copy(m_in.at[:, pl.ds(1024, 256)], m_box.at[1, fs], m_send.at[1, dy], m_recv.at[1, fs], there),
        )

    def m_arrival(j):
        there = dev(xh, fs, z, j)
        return [
            copy(m_in.at[:, pl.ds(1024, 256)], m_box.at[half, j], m_send.at[half, 0], m_recv.at[half, j], there)
            for half in range(2)
        ]

    for dy in range(1, 4):
        for one in m_copy(dy):
            one.start()

    @pl.when(fs != y)
    def _():
        for one in m_copy(0):
            one.start()

    @pl.when(fs == y)
    def _():
        m_box[0, fs] = m_in[:, pl.ds(pl.multiple_of(y * 256, 256), 256)]
        m_box[1, fs] = m_in[:, 1024:1280]

    sibling = dev(xh, y, z, xlo * 2 + 1 - core)
    spot = xh * 2 + xlo

    def n_copy(dx, to):
        other = (spot + dx) % 4 if to else (spot + 4 - dx) % 4
        oxh, ofs = other // 2, other % 2 * 2 + core
        slot = member if to else oxh * 4 + ofs
        return copy(normed_all.at[member], normed_all.at[slot], n_send.at[dx], n_recv.at[dx], dev(oxh, y, z, ofs))

    def n_share(dx, to):
        other = (spot + 4 - dx) % 4
        slot = other // 2 * 4 + other % 2 * 2 + (core if to else 1 - core)
        return copy(normed_all.at[slot], normed_all.at[slot], n_send.at[4 + dx], n_recv.at[4 + dx], sibling)

    def g_copy(step, to):
        dx, df = step // 4, step % 4
        oxh = (xh + dx) % 2
        ofs = (fs + df) % 4 if to else (fs + 4 - df) % 4
        slot = member if to else oxh * 4 + ofs
        return copy(seg_in, seg_all.at[slot], g_send.at[step], g_recv.at[step], dev(oxh, y, z, ofs))

    for dx in (1, 3, 2):
        n_copy(dx, True).start()
    n_share(0, True).start()
    for step in range(1, 8):
        g_copy(step, True).start()

    def ten(count, depth):
        place = lax.broadcasted_iota(jnp.int32, (count, depth), 0)
        column = lax.broadcasted_iota(jnp.int32, (count, depth), 1)
        tens = (place * 52429) >> 19
        return jnp.where(column == tens * 16 + (place - tens * 10), 1.0, 0.0).astype(bf)

    def settle(picker, block):
        return mix(picker, block).astype(bf)

    pick80 = ten(80, 128)
    for step in range(1, 8):
        q_arrival(step).wait_recv()
    wq[z] = settle(pick80, q_box[...].reshape(128, 512))

    last = (8, 7)
    o_tile = y + y // 2
    o_part = pl.ds(pl.multiple_of(o_tile * 128, 128), 128)
    m_part = pl.ds(pl.multiple_of(y * 256, 256), 256)
    views = (
        lambda src: wq.at[src],
        lambda src: wo.at[core, src, :, o_part],
        lambda src: wo.at[core, src, :, pl.ds(256, 128)],
        lambda src: wm.at[src, :, m_part],
        lambda src: wm.at[src, :, pl.ds(1024, 256)],
        lambda src: slots.at[src],
    )

    def block_at(way, gone):
        return (z + NZ - gone) % NZ if way == 0 else (z + gone) % NZ

    def ring(k, way, step, arriving):
        view = views[k](block_at(way, step if arriving else step - 1))
        where = dev(xh, y, up if way == 0 else below, fs)
        return copy(view, view, c_send.at[k, way, step - 1], c_recv.at[k, way, step - 1], where)

    def begin(k):
        for way in range(2):
            ring(k, way, 1, False).start()

    def share(half, place, slot):
        return copy(wo.at[half, place], wo.at[half, place], s_send.at[slot], s_recv.at[slot], sibling)

    def o_along(place, slot, dy, to):
        oy = (y + dy) % 4 if to else (y + 4 - dy) % 4
        part = o_part if to else pl.ds(pl.multiple_of((oy + oy // 2) * 128, 128), 128)
        view = wo.at[core, place, :, part]
        return copy(view, view, y_send.at[slot, dy - 1], y_recv.at[slot, dy - 1], dev(xh, oy, z, fs))

    def m_along(place, slot, dy, to):
        oy = (y + dy) % 4 if to else (y + 4 - dy) % 4
        part = m_part if to else pl.ds(pl.multiple_of(oy * 256, 256), 256)
        view = wm.at[place, :, part]
        return copy(view, view, y_send.at[slot, dy + 2], y_recv.at[slot, dy + 2], dev(xh, oy, z, fs))

    def places(step):
        if step == 0:
            return [(z, 0)]
        return [(block_at(way, step), step + 8 * way) for way in range(2) if step <= last[way]]

    def serve(step):
        for k in (0, 1, 3, 2, 4, 5):
            for way in range(2):
                if step <= last[way]:
                    ring(k, way, step, True).wait_recv()
                    if step < last[way]:
                        ring(k, way, step + 1, False).start()

    def spread_out(step):
        for place, slot in places(step):
            for dy in (1, 3, 2):
                o_along(place, slot, dy, True).start()
        for place, slot in places(step):
            for dy in (1, 3, 2):
                m_along(place, slot, dy, True).start()

    def pass_on(step):
        for place, slot in places(step):
            for dy in range(1, 4):
                o_along(place, slot, dy, False).wait_recv()
            share(core, place, slot).start()

    begin(0)
    begin(5)
    for c in range(2):
        for k in range(16):
            dx, dl, dy = o_steps[k]
            here = (core + dl) % 2 == xlo
            cond = here if dx or dy else here & (core * 2 + c != fs)

            @pl.when(cond)
            def _():
                o_arrival(c, k).wait_recv()
    wo[core, z, :, 256:384] = settle(pick80, (o_box[0, :, :, 256:384] + o_box[1, :, :, 0:128]).reshape(128, 128))
    from_lane = pl.ds(pl.multiple_of((y % 2 + y // 2) * 128, 128), 128)
    wo[core, z, :, o_part] = settle(pick80, o_box[y // 2, :, :, from_lane].reshape(128, 128))
    begin(1)
    begin(2)
    for j in range(4):
        @pl.when((j != fs) | (y != fs))
        def _():
            for one in m_arrival(j):
                one.wait_recv()
    pick40 = ten(40, 64)
    wm[z, :, m_part] = settle(pick40, m_box[0].reshape(64, 256))
    wm[z, :, 1024:1280] = settle(pick40, m_box[1].reshape(64, 256))
    begin(3)
    begin(4)
    spread_out(0)
    tok_t[...] = mix_t(unmove[...], tok_in[...]).astype(bf)

    for step in range(1, 9):
        serve(step)
        spread_out(step)
        if step > 1:
            pass_on(step - 2)
        if step == 4:
            for dx in (1, 3):
                n_copy(dx, False).wait_recv()
                n_share(dx, True).start()
        if step == 6:
            n_copy(2, False).wait_recv()
            n_share(2, True).start()
    for dx in range(4):
        n_share(dx, False).wait_recv()
    for step in range(1, 8):
        g_copy(step, False).wait_recv()

    factor = 1.0 / math.sqrt(HD)

    def a_copy(step, to):
        dx, df = step // 4, step % 4
        oxh = (xh + dx) % 2
        ofs = (fs + df) % 4 if to else (fs + 4 - df) % 4
        head = fs * 2 + xh if to else ofs * 2 + oxh
        return copy(
            att_out.at[oxh * 4 + ofs], att_in.at[rows_of(head, 160), :], a_send.at[step], a_recv.at[step], dev(oxh, y, z, ofs)
        )

    def project(g):
        block = normed_all[pl.ds(g * 4, 4)].reshape(512, 1280)
        qkv[...] = mix(block, wq[...].reshape(1280, 512)).astype(bf)

    def attend(g):
        names = [seg_all[g * 4 + b][0:1, :].astype(jnp.float32) for b in range(4)]
        downs = [jnp.concatenate([jnp.broadcast_to(one, (128, 128)).T] * 4, axis=1) for one in names]
        allowed = jnp.concatenate(downs, axis=0) == jnp.concatenate(names, axis=1)
        for h in range(2):
            query = qkv[:, h * HD : h * HD + HD]
            key = qkv[:, 160 + h * HD : 160 + h * HD + HD]
            value = qkv[:, 320 + h * HD : 320 + h * HD + HD]
            scores = jnp.where(allowed, mix_t(key, query) * factor, -jnp.inf)
            weights = jnp.exp(scores - jnp.max(scores, axis=0, keepdims=True))
            totals = jnp.sum(weights, axis=0, keepdims=True)
            value_t = value.astype(jnp.float32).T.astype(bf)
            head_out = (mix(value_t, weights.astype(bf)) / totals).astype(bf)
            for b in range(4):
                att_out[g * 4 + b, h * HD : h * HD + HD, :] = head_out[:, b * 128 : (b + 1) * 128]

    project(1 - xh)
    attend(1 - xh)
    for step in range(4, 8):
        a_copy(step, True).start()
    project(xh)
    attend(xh)
    att_in[rows_of(fs * 2 + xh, 160), :] = att_out[member]
    for step in range(1, 4):
        a_copy(step, True).start()
    pass_on(7)
    pass_on(8)
    for step in range(1, 8):
        a_copy(step, False).wait_recv()
    for step in range(9):
        for place, slot in places(step):
            share(1 - core, place, slot).wait_recv()

    update = mix(wo[0].reshape(1280, 640), att_in[0:640, :]) + mix(wo[1].reshape(1280, 640), att_in[640:1280, :])
    layer_t = (tok_t[...].astype(jnp.float32) + update).astype(bf)
    down = lax.broadcasted_iota(jnp.int32, (128, 128), 0)
    named = jnp.where(order_row[...] == down, 1.0, 0.0).astype(bf)
    regular = jnp.where(lane == ((down & 31) << 2) + (down >> 5), 1.0, 0.0).astype(bf)
    picker = mix_t(regular, named).astype(bf)
    chosen = mix_t(picker, layer_t).astype(bf)
    merge_in = (center(mix(chosen, unmove[...])) * gain_in[1:2, :]).astype(bf)
    for b in range(8):
        mi_out[b] = merge_in[b // 2 * 32 : b // 2 * 32 + 32, b % 2 * 640 : b % 2 * 640 + 640]

    def i_copy(step, to):
        dx, df = step // 4, step % 4
        oxh = (xh + dx) % 2
        ofs = (fs + df) % 4 if to else (fs + 4 - df) % 4
        other = oxh * 4 + ofs
        slot = member if to else other
        return copy(mi_out.at[other], mi_in.at[slot], i_send.at[step], i_recv.at[step], dev(oxh, y, z, ofs))

    for step in range(1, 8):
        i_copy(step, True).start()
    mi_in[member] = mi_out[member]
    for step in range(9):
        for place, slot in places(step):
            for dy in range(1, 4):
                m_along(place, slot, dy, False).wait_recv()
    for step in range(1, 8):
        i_copy(step, False).wait_recv()

    def t_copy(c):
        return copy(pair_out.at[c], pair_in.at[c], t_send.at[c], t_recv.at[c], sibling)

    def r_copy(c, dx, to):
        other = (spot + dx) % 4 if to else (spot + 4 - dx) % 4
        slot = spot if to else other
        there = dev(other // 2, y, z, other % 2 * 2 + core)
        return copy(part_out.at[c, other], part_in.at[c, slot], r_send.at[c, dx], r_recv.at[c, dx], there)

    inputs = mi_in[...].reshape(256, 640)
    for c in range(CH):
        part_f[c] = mix(inputs, wm[:, :, c * CW : (c + 1) * CW].reshape(640, CW)).reshape(4, 2, 32, CW)
        for s in range(4):
            pair_out[c, s] = part_f[c, s, 1 - core].astype(bf)
        t_copy(c).start()
    for c in range(CH):
        t_copy(c).wait_recv()
        for s in range(4):
            part_out[c, s] = (part_f[c, s, core] + pair_in[c, s].astype(jnp.float32)).astype(bf)
        for dx in (2, 1, 3):
            r_copy(c, dx, True).start()
        part_in[c, spot] = part_out[c, spot]

    def seat(way, gone):
        return 0 if gone == 0 else 15 if gone == 8 else 2 * gone - 1 + way

    def e_copy(c, way, step):
        where = dev(xh, y, up if way == 0 else below, fs)
        return copy(
            rows.at[c, seat(way, step - 1)], rows.at[c, seat(way, step)], e_send.at[c, way, step - 1], e_recv.at[c, way, step - 1], where
        )

    for c in range(CH):
        for dx in range(1, 4):
            r_copy(c, dx, False).wait_recv()
        rows[c, 0] = jnp.sum(part_in[c].astype(jnp.float32), axis=0).astype(bf)
        for way in range(2):
            e_copy(c, way, 1).start()

    parts = ((0, 8, 4), (8, 4, 6), (12, 4, 8))
    boxes = ((picked1, landed1), (picked2, landed2), (picked3, landed3))

    def p_copy(part, c, step, to):
        dx, dy = step // 4, step % 4
        oxh = (xh + dx) % 2
        oy = (y + dy) % 4 if to else (y + 4 - dy) % 4
        other = oxh * 4 + oy
        slot = mine if to else other
        gone, come = boxes[part]
        return copy(
            gone.at[c, other], come.at[c, slot], p_send.at[part, c, step], p_recv.at[part, c, step], dev(oxh, oy, z, fs)
        )

    row_keys = []
    lane_row = lax.broadcasted_iota(jnp.int32, (1, 128), 1)
    for q in range(4):
        row_key = jnp.zeros((1, 128), jnp.int32)
        for i in range(4):
            number = 4 * q + i
            gone = (number + 1) // 2
            source = block_at(0, gone) if number % 2 else block_at(1, gone)
            row_key = jnp.where((lane_row >> 5) == i, slots[source][0:1, :], row_key)
        row_keys.append(row_key)
    selects, turns = [], []
    for first, count, _ in parts:
        shape = (16 * count, 32 * count)
        bits = 4 if count == 8 else 3
        place = lax.broadcasted_iota(jnp.int32, shape, 0)
        column = lax.broadcasted_iota(jnp.int32, shape, 1)
        wanted = ((place >> bits) << 5) + 2 * z + (place & 1) + 1
        keys = jnp.concatenate(row_keys[first // 4 : (first + count) // 4], axis=1)
        match = (((place >> 1) & (count - 1)) == (column >> 5)) & (keys == wanted)
        selects.append(jnp.where(match, 1.0, 0.0).astype(bf))
        shape = (256, 16 * count)
        place = lax.broadcasted_iota(jnp.int32, shape, 0)
        column = lax.broadcasted_iota(jnp.int32, shape, 1)
        number = ((column >> 1) & (count - 1)) + first
        gone = (number + 1) >> 1
        source = (z + jnp.where((number & 1) == 1, NZ - gone, gone)) & 15
        match = ((place >> 5) == (column >> bits)) & ((place & 1) == (column & 1)) & (((place >> 1) & 15) == source)
        turns.append(jnp.where(match, 1.0, 0.0).astype(bf))
    for step in range(1, 9):
        for c in range(CH):
            for way in range(2):
                if step <= last[way]:
                    e_copy(c, way, step).wait_recv()
                    if step < last[way]:
                        e_copy(c, way, step + 1).start()
            if step == 8:
                first, count, _ = parts[2]
                block = mix(selects[2], rows[c, first : first + count].reshape(32 * count, CW)).astype(bf)
                boxes[2][0][c] = block.reshape(8, 2 * count, CW)
                for hop in range(1, 8):
                    p_copy(2, c, hop, True).start()
        for part in range(2):
            first, count, ready = parts[part]
            if step == ready:
                for c in range(CH):
                    block = mix(selects[part], rows[c, first : first + count].reshape(32 * count, CW)).astype(bf)
                    boxes[part][0][c] = block.reshape(8, 2 * count, CW)
                    for hop in range(1, 8):
                        p_copy(part, c, hop, True).start()
    for c in range(CH):
        total = None
        for part in range(3):
            gone, come = boxes[part]
            come[c, mine] = gone[c, mine]
            for step in range(1, 8):
                p_copy(part, c, step, False).wait_recv()
            block = mix(turns[part], come[c].reshape(16 * parts[part][1], CW))
            total = block if total is None else total + block
        out[:, c * CW : (c + 1) * CW] = total.astype(bf)

    for step in range(1, 8):
        q_copy(step).wait_send()
        g_copy(step, True).wait_send()
        a_copy(step, True).wait_send()
        i_copy(step, True).wait_send()
        for c in range(CH):
            for part in range(3):
                p_copy(part, c, step, True).wait_send()
    for c in range(CH):
        t_copy(c).wait_send()
        for dx in range(1, 4):
            r_copy(c, dx, True).wait_send()
    for dx in range(4):
        n_share(dx, True).wait_send()
        if dx:
            n_copy(dx, True).wait_send()
    for k in range(16):
        cond = o_remote(k)
        if cond is None:
            o_copy(k).wait_send()
        else:
            @pl.when(cond)
            def _():
                o_copy(k).wait_send()
    for dy in range(1, 4):
        for one in m_copy(dy):
            one.wait_send()

    @pl.when(fs != y)
    def _():
        for one in m_copy(0):
            one.wait_send()

    for way in range(2):
        for step in range(1, last[way] + 1):
            for k in range(6):
                ring(k, way, step, False).wait_send()
            for c in range(CH):
                e_copy(c, way, step).wait_send()
    for step in range(9):
        for place_, slot in places(step):
            share(core, place_, slot).wait_send()
            for dy in range(1, 4):
                o_along(place_, slot, dy, True).wait_send()
                m_along(place_, slot, dy, True).wait_send()


def block(*operands):
    bf = jnp.bfloat16
    dma = pltpu.SemaphoreType.DMA
    vm = pltpu.VMEM
    return pl.pallas_call(
        block_kernel,
        out_shape=jax.ShapeDtypeStruct((256, 1280), bf),
        in_specs=[pl.BlockSpec(memory_space=pltpu.VMEM)] * 8,
        out_specs=pl.BlockSpec(memory_space=pltpu.VMEM),
        scratch_shapes=[
            vm((8, 128), jnp.int32), vm((NZ, 80, 512), bf), vm((2, NZ, 80, 640), bf), vm((NZ, 40, 1280), bf), vm((1280, 1280), bf),
            vm((1280, 128), bf), vm((8, 128, 1280), bf), vm((8, 8, 128), jnp.int32),
            vm((8, 16, 512), bf), vm((2, 8, 16, 384), bf), vm((2, 4, 16, 256), bf), vm((NZ, 8, 128), jnp.int32),
            vm((512, 512), bf), vm((8, 160, 128), bf), vm((1280, 128), bf), vm((8, 32, 640), bf), vm((8, 32, 640), bf),
            vm((CH, 4, 32, CW), bf), vm((CH, 4, 32, CW), bf), vm((CH, NZ, 32, CW), bf),
            vm((CH, 8, 16, CW), bf), vm((CH, 8, 8, CW), bf), vm((CH, 8, 8, CW), bf), vm((CH, 8, 16, CW), bf), vm((CH, 8, 8, CW), bf), vm((CH, 8, 8, CW), bf),
            vm((CH, 4, 2, 32, CW), jnp.float32), vm((CH, 4, 32, CW), bf), vm((CH, 4, 32, CW), bf), dma((CH,)), dma((CH,)),
            dma((6, 2, 8)), dma((6, 2, 8)), dma((17, 6)), dma((17, 6)), dma((CH, 2, 8)), dma((CH, 2, 8)),
            dma((8,)), dma((8,)), dma((16,)), dma((2, 16)), dma((2, 4)), dma((2, 4)),
            dma((8,)), dma((8,)), dma((8,)), dma((8,)),
            dma((17,)), dma((17,)), dma((8,)), dma((8,)), dma((8,)), dma((8,)),
            dma((CH, 8)), dma((CH, 8)), dma((3, CH, 8)), dma((3, CH, 8)),
        ],
        compiler_params=pltpu.CompilerParams(collective_id=1, has_side_effects=True, vmem_limit_bytes=60 << 20),
    )(*operands)


def per_device(
    tokens, qkv_weight, out_weight, merge_weight, ln_gains, segments, merge_rows, owners
):
    fs = lax.axis_index("fsdp")
    q_in = qkv_weight.reshape(3, 10, 2, 160).transpose(2, 1, 0, 3).reshape(2, 10, 480)
    q_in = jnp.pad(q_in, ((0, 0), (0, 6), (0, 32)))
    o_flat = out_weight.T
    o_in = jnp.where(fs % 2 == 0, jnp.pad(o_flat, ((0, 6), (0, 64))), jnp.pad(o_flat, ((0, 6), (64, 0))))
    m_in = jnp.pad(merge_weight, ((0, 6), (0, 0)))
    return block(tokens, ln_gains, q_in, o_in, m_in, segments, merge_rows, owners)


def solution(mesh):
    cut = Mesh(mesh.devices.reshape(2, 64, 4), ("xh", "yz", "fsdp"))
    every = ("xh", "yz", "fsdp")
    return jax.shard_map(
        per_device,
        mesh=cut,
        in_specs=(
            P(every, None),
            P(None, ("xh", "yz"), "fsdp"),
            P("fsdp", ("xh", "yz")),
            P(every, None),
            P(),
            P(("xh", "yz"), "fsdp"),
            P(every, None),
            P(every, None),
        ),
        out_specs=P(every, None),
        check_vma=False,
    )
```
